32 devices in a mesh: chain: 4 (over x, core), col: 8 (over z, y).
Axes of the slice: x: 2, y: 2, z: 4, core: 2. Of those that a mesh axis runs over, the one named last changes fastest.
Arguments:
- rhs: float32 [4, 8, 64, 128], P('chain', 'col'), may hold values from -6 to 6
- inverse: float32 [4, 8, 128, 128], P('chain', 'col'), as said below
- factor: float32 [4, 8, 8, 128, 128], P('chain', 'col'), may hold values from -0.1875 to 0.1875
- pattern: int32 [4, 8, 8], P('chain', 'col'), may hold values from 0 to 7, as said below
Outputs:
- forward: float32 [4, 8, 64, 128], P('chain', 'col')
- solution: float32 [4, 8, 64, 128], P('chain', 'col')
The draws below stay inside these ranges and needn't reach their ends.
Inputs may be any that keep to these rules, and one draw needn't show every extreme that they name: `pattern`: the 8 block rows of one supernode are distinct. `inverse`: each block is lower triangular, its diagonal between 0.5 and 1.5.
All inputs are finite; a program needn't handle non-finite values.
Results may differ from the reference program's by a relative error of at most 0.00012.
Values sent between devices are 32-bit elements; how exact they have to be, the bound alone decides.
A program may use at most 64 MiB of HBM per device.

```python
import jax
import jax.numpy as jnp
from jax import lax

BLOCK = 128
NB = 8
LOADS = 64
LEVELS = 4
SUPS = 8


def draw_inverse(key, part):
    keyed = jax.random.fold_in(key, 7)
    first, second = jax.random.split(keyed)
    diagonal = jax.random.uniform(first, (LEVELS, SUPS, BLOCK), jnp.float32, 0.5, 1.5)
    lower = jax.random.normal(second, (LEVELS, SUPS, BLOCK, BLOCK), jnp.float32) * (0.6 / BLOCK ** 0.5)
    strict = jnp.tril(jnp.ones((BLOCK, BLOCK), jnp.float32), -1)
    return lower * strict + diagonal[..., None] * jnp.eye(BLOCK, dtype=jnp.float32)


def draw_pattern(key, part):
    keyed = jax.random.fold_in(key, 11)
    keys = jax.random.split(keyed, LEVELS * SUPS)
    chosen = jax.vmap(lambda single: jax.random.permutation(single, SUPS)[:NB])(keys)
    return chosen.reshape(LEVELS, SUPS, NB).astype(jnp.int32)


def block_levels(own_key, extent, cuts, smallest, high):
    gain = 1.0
    for axis_at, shards_of in cuts:
        draws = jax.random.uniform(jax.random.fold_in(jax.random.fold_in(own_key, 6), axis_at), (shards_of,), jnp.float32, smallest / len(cuts), high / len(cuts))
        gain = gain * jnp.repeat(jnp.exp(draws), extent[axis_at] // shards_of).reshape((-1,) + (1,) * (len(extent) - 1 - axis_at))
    return gain


def bell_draw(key, dims, scale, limit, shards=(), kind=jnp.bfloat16):
    loudness = block_levels(key, dims, shards, -0.22, 0.18) if shards else 1.0
    values = jax.random.normal(key, dims, jnp.float32) * scale * loudness
    return jnp.minimum(jnp.maximum(values, -limit), limit).astype(kind)


def setup_inputs(seed: int = 0) -> dict:
    key_list = jax.random.split(jax.random.key(seed), 5)
    return {
        "rhs": bell_draw(key_list[0], (LEVELS, SUPS, LOADS, BLOCK), 1.0, 6.0, ((0, 4), (1, 8)), jnp.float32),
        "inverse": draw_inverse(jax.random.fold_in(key_list[4], 71), 0),
        "factor": bell_draw(key_list[2], (LEVELS, SUPS, NB, BLOCK, BLOCK), (BLOCK * NB) ** -0.5, 0.1875, ((0, 4), (1, 8)), jnp.float32),
        "pattern": draw_pattern(jax.random.fold_in(key_list[4], 71), 0),
    }


def reference(rhs, inverse, factor, pattern):
    highest = lax.Precision.HIGHEST
    onehot = (pattern[..., None] == jnp.arange(SUPS, dtype=jnp.int32)).astype(jnp.float32)
    incoming = jnp.zeros((SUPS, LOADS, BLOCK), jnp.float32)
    forward_list = []
    for level in range(LEVELS):
        solved = jnp.einsum("jrb,jab->jra", rhs[level] - incoming, inverse[level], precision=highest)
        forward_list.append(solved)
        terms = jnp.einsum("jrb,jkab->jkra", solved, factor[level], precision=highest)
        incoming = jnp.einsum("jkc,jkra->cra", onehot[level], terms, precision=highest)
    outgoing = jnp.zeros((SUPS, LOADS, BLOCK), jnp.float32)
    solution_list = [None] * LEVELS
    for level in reversed(range(LEVELS)):
        solved = jnp.einsum("jra,jab->jrb", forward_list[level] - outgoing, inverse[level], precision=highest)
        solution_list[level] = solved
        if level > 0:
            picked = jnp.einsum("jkc,cra->jkra", onehot[level - 1], solved, precision=highest)
            outgoing = jnp.einsum("jkra,jkab->jrb", picked, factor[level - 1], precision=highest)
    return jnp.stack(forward_list), jnp.stack(solution_list)
```

```python
import functools

import jax
import jax.numpy as jnp
from jax import lax
from jax.experimental import pallas as pl
from jax.experimental.pallas import tpu as pltpu
from jax.sharding import PartitionSpec as P

PIECES = 4
MESH = pl.DeviceIdType.MESH


def halves(value):
    high = value.astype(jnp.bfloat16)
    low = (value - high.astype(jnp.float32)).astype(jnp.bfloat16)
    return high, low


def times_transposed(value, packed):
    rows = value.shape[0]
    high, low = halves(value)
    stacked = jnp.concatenate(
        [jnp.concatenate([high, low], axis=1), jnp.concatenate([low, high], axis=1)], axis=0
    )
    both = lax.dot_general(
        stacked, packed, (((1,), (1,)), ((), ())), preferred_element_type=jnp.float32
    )
    return both[:rows] + both[rows:]


def times_turned(value, turned):
    rows = value.shape[0]
    high, low = halves(value)
    stacked = jnp.concatenate(
        [jnp.concatenate([high, low], axis=1), jnp.concatenate([low, high], axis=1)], axis=0
    )
    both = jnp.dot(stacked, turned, preferred_element_type=jnp.float32)
    return both[:rows] + both[rows:]


def times(value, packed):
    rows = value.shape[0]
    width = packed.shape[1] // 2
    high, low = halves(value)
    both = jnp.dot(
        jnp.concatenate([high, low], axis=0), packed, preferred_element_type=jnp.float32
    )
    summed = both[:rows] + both[rows:]
    return summed[:, :width] + summed[:, width:]


def kernel(
    levels, supers, rhs_hbm, inverse_hbm, factor_hbm, pattern_hbm, both_ref,
    rhs, inverse, factor, pattern, inverse_packed, packed, turned, terms, outbox, inbox, solved,
    load_sem, outbox_sem, inbox_sem, solved_sem, arrived_sem, *arrived,
):
    forward_ref, answer_ref = both_ref.at[0], both_ref.at[1]
    place = lax.axis_index("chain")
    me = lax.axis_index("col")
    count, _, width = factor.shape
    loads = rhs.shape[0]
    rows = loads // PIECES
    loading = [
        pltpu.make_async_copy(source, target, load_sem.at[at])
        for at, (source, target) in enumerate(
            ((rhs_hbm, rhs), (inverse_hbm, inverse), (factor_hbm, factor), (pattern_hbm, pattern))
        )
    ]
    for copy in loading:
        copy.start()
    peers = [lax.rem(me + shift, supers) for shift in range(supers)]

    barrier = pltpu.get_barrier_semaphore()

    @pl.when(place > 0)
    def _():
        for peer in peers:
            pl.semaphore_signal(
                barrier, inc=1, device_id={"chain": place - 1, "col": peer}, device_id_type=MESH
            )

    @pl.when(place < levels - 1)
    def _():
        for peer in peers:
            pl.semaphore_signal(
                barrier, inc=1, device_id={"chain": place + 1, "col": peer}, device_id_type=MESH
            )

    loading[0].wait()
    loading[1].wait()
    high, low = halves(inverse[...])
    inverse_packed[:, :width] = high
    inverse_packed[:, width:] = low

    full = count == supers

    def pack(block, value):
        high, low = halves(value)
        packed[block * width:(block + 1) * width, :width] = high
        packed[block * width:(block + 1) * width, width:] = low

    def pack_turned(block, value):
        high, low = halves(value.T)
        turned[:width, block * width:(block + 1) * width] = high
        turned[width:, block * width:(block + 1) * width] = low

    def block_of(block):
        return factor[jnp.maximum(origin[block], 0)] if full else factor[block]

    loading[2].wait()
    loading[3].wait()
    targets = [pattern[0, 0, block] for block in range(count)]
    origin = []
    for peer in peers:
        at = jnp.int32(-1)
        for block in range(count):
            at = jnp.where(targets[block] == peer, jnp.int32(block), at)
        origin.append(at)
    slots = [lax.rem(me - target + supers, supers) for target in targets]

    @pl.when(place == 0)
    def _():
        for block in range(count):
            pack_turned(block, block_of(block))
        rhs[...] = times_transposed(rhs[...], inverse_packed[...])
        forward_ref[...] = rhs[...]

    @pl.when((place > 0) & (place < levels - 1))
    def _():
        for block in range(count):
            product = times(block_of(block), inverse_packed[...])
            pack(block, product)
            pack_turned(block, product)

    @pl.when(place == levels - 1)
    def _():
        pack(0, times(inverse[...].T, inverse_packed[...]))

    def term_copy(piece, shift):
        return pltpu.make_async_remote_copy(
            src_ref=outbox.at[piece, shift],
            dst_ref=inbox.at[piece, shift],
            send_sem=outbox_sem.at[piece, shift],
            recv_sem=inbox_sem.at[piece],
            device_id={"chain": place + 1, "col": peers[shift]},
            device_id_type=MESH,
        )

    def answer_copy(piece, shift):
        return pltpu.make_async_remote_copy(
            src_ref=solved.at[piece],
            dst_ref=arrived[piece].at[shift],
            send_sem=solved_sem.at[piece, shift],
            recv_sem=arrived_sem.at[piece],
            device_id={"chain": place - 1, "col": peers[shift]},
            device_id_type=MESH,
        )

    for piece in range(PIECES):
        part = pl.ds(piece * rows, rows)

        @pl.when(place > 0)
        def _():
            pltpu.make_async_copy(inbox.at[piece], inbox.at[piece], inbox_sem.at[piece]).wait()
            total = rhs[part, :] - jnp.sum(inbox[piece], axis=0)
            rhs[part, :] = total

        @pl.when(place < levels - 1)
        def _():
            wide = times_turned(rhs[part, :], turned[...])
            if full:
                for shift in range(supers):
                    outbox[piece, shift] = wide[:, shift * width:(shift + 1) * width]
            else:
                for block in range(count):
                    terms[block] = wide[:, block * width:(block + 1) * width]
                for shift in range(supers):
                    picked = terms[jnp.maximum(origin[shift], 0)]
                    outbox[piece, shift] = jnp.where(origin[shift] >= 0, picked, 0.0)

        @pl.when(place == levels - 1)
        def _():
            fresh = times(rhs[part, :], packed[:width, :])
            solved[piece] = fresh
            answer_ref[part, :] = fresh

        if piece == 0:
            pl.semaphore_wait(
                barrier, jnp.where(place > 0, supers, 0) + jnp.where(place < levels - 1, supers, 0)
            )

        @pl.when(place < levels - 1)
        def _():
            for shift in range(supers):
                term_copy(piece, shift).start()

        @pl.when(place == levels - 1)
        def _():
            for shift in range(supers):
                answer_copy(piece, shift).start()

    @pl.when(place > 0)
    def _():
        forward_ref[...] = times_transposed(rhs[...], inverse_packed[...])

    @pl.when(place == 0)
    def _():
        for block in range(count):
            pack(block, times(block_of(block), inverse_packed[...]))

    @pl.when(place < levels - 1)
    def _():
        rhs[...] = times(forward_ref[...], inverse_packed[...])
        for piece in range(PIECES):
            part = pl.ds(piece * rows, rows)
            pltpu.make_async_copy(arrived[piece], arrived[piece], arrived_sem.at[piece]).wait()
            if full:
                chosen = [arrived[piece][(supers - shift) % supers] for shift in range(supers)]
            else:
                chosen = [arrived[piece][slot] for slot in slots]
            picked = jnp.concatenate(chosen, axis=1)
            fresh = rhs[part, :] - times(picked, packed[...])
            solved[piece] = fresh
            answer_ref[part, :] = fresh

            @pl.when(place > 0)
            def _():
                for shift in range(supers):
                    answer_copy(piece, shift).start()

    @pl.when(place < levels - 1)
    def _():
        for piece in range(PIECES):
            for shift in range(supers):
                term_copy(piece, shift).wait_send()

    @pl.when(place > 0)
    def _():
        for piece in range(PIECES):
            for shift in range(supers):
                answer_copy(piece, shift).wait_send()


def body(rhs, inverse, factor, pattern):
    levels = lax.axis_size("chain")
    supers = lax.axis_size("col")
    loads, width = rhs.shape[2:]
    count = factor.shape[2]
    rows = loads // PIECES
    block = pltpu.VMEM((2, loads, width), jnp.float32)
    anywhere = pl.BlockSpec(memory_space=pl.ANY)
    both = pl.pallas_call(
        functools.partial(kernel, levels, supers),
        out_shape=block,
        in_specs=[anywhere] * 4,
        out_specs=pl.BlockSpec(memory_space=pltpu.VMEM),
        scratch_shapes=[
            pltpu.VMEM((loads, width), jnp.float32),
            pltpu.VMEM((width, width), jnp.float32),
            pltpu.VMEM((count, width, width), jnp.float32),
            pltpu.SMEM((1, 1, count), jnp.int32),
            pltpu.VMEM((width, 2 * width), jnp.bfloat16),
            pltpu.VMEM((count * width, 2 * width), jnp.bfloat16),
            pltpu.VMEM((2 * width, count * width), jnp.bfloat16),
            pltpu.VMEM((count, rows, width), jnp.float32),
            pltpu.VMEM((PIECES, supers, rows, width), jnp.float32),
            pltpu.VMEM((PIECES, supers, rows, width), jnp.float32),
            pltpu.VMEM((PIECES, rows, width), jnp.float32),
            pltpu.SemaphoreType.DMA((4,)),
            pltpu.SemaphoreType.DMA((PIECES, supers)),
            pltpu.SemaphoreType.DMA((PIECES,)),
            pltpu.SemaphoreType.DMA((PIECES, supers)),
            pltpu.SemaphoreType.DMA((PIECES,)),
            *[pltpu.VMEM((supers, rows, width), jnp.float32)] * PIECES,
        ],
        compiler_params=pltpu.CompilerParams(collective_id=0, has_side_effects=True),
    )(rhs[0, 0], inverse[0, 0], factor[0, 0], pattern)
    return (both[None, :1], both[None, 1:])


def spread_kernel(
    supers, rhs_hbm, inverse_hbm, factor_hbm, pattern_hbm, both_ref,
    rhs, inverse, factor, pattern, inverse_packed, packed, turned,
    made, near1, near2, square1, square2, square3, side1, side2, side3,
    turned1, packed1, turned2, packed2, mean1, mean2, mean3,
    outbox, inbox1, inbox2, inbox3, inbox4, inbox5, held1, held2, held3, kept1, kept2, solved2, solved3,
    back_u, back_x, back_pair,
    load_sem, send_sem, near1_sem, near2_sem, square_sem, side_sem,
    sem1, sem2, sem3, sem4, sem5, back_sem,
):
    forward_ref, answer_ref = both_ref.at[0], both_ref.at[1]
    place = lax.axis_index("chain")
    me = lax.axis_index("col")
    depth = supers // 2
    z, y = lax.div(me, 2), lax.rem(me, 2)
    other = 1 - y
    width = factor.shape[1]
    rows = inbox1.shape[3]
    half = 2 * rows
    sends = []
    count = send_sem.shape[0]
    free = [None]
    later = [None, None]

    def at(chain, deep, side):
        return {"chain": chain, "col": 2 * deep + side}

    def remote(build, wanted=None):
        index = next(free[0])

        def make():
            source, target, arrival, device = build()
            return pltpu.make_async_remote_copy(
                src_ref=source, dst_ref=target, send_sem=send_sem.at[index], recv_sem=arrival,
                device_id=device, device_id_type=MESH,
            )

        if wanted is None:
            make().start()
        else:
            pl.when(wanted())(lambda: make().start())
        sends.append((make, wanted))

    def take():
        taken = list(sends)
        sends.clear()
        return taken

    def finish(taken):
        for make, wanted in taken:
            if wanted is None:
                make().wait_send()
            else:
                pl.when(wanted())(lambda make=make: make().wait_send())

    def arrive(ref, sem):
        pltpu.make_async_copy(ref, ref, sem).wait()

    def rest(count):
        step = 1 - 2 * lax.div(z, depth // 2)
        return [lax.rem(z + step * k + count, count) for k in reversed(range(count))]

    far = rest(depth)

    def pack_into(ref, row, column, columns, value):
        high, low = halves(value)
        ref[row * width:(row + 1) * width, column * width:(column + 1) * width] = high
        ref[row * width:(row + 1) * width, (columns + column) * width:(columns + column + 1) * width] = low

    loading = [
        pltpu.make_async_copy(source, target, load_sem.at[index])
        for index, (source, target) in enumerate(
            ((rhs_hbm, rhs), (inverse_hbm, inverse), (factor_hbm, factor), (pattern_hbm, pattern))
        )
    ]
    for copy in loading:
        copy.start()

    barrier = pltpu.get_barrier_semaphore()

    def greet(device, wanted=None):
        def go():
            pl.semaphore_signal(barrier, inc=1, device_id=device, device_id_type=MESH)

        if wanted is None:
            go()
        else:
            pl.when(wanted)(go)

    @pl.when(place < 2)
    def _():
        for shift in range(supers):
            peer = lax.rem(me + shift, supers)
            greet({"chain": 0, "col": peer}, None if shift else place > 0)
        greet(at(1, z, other))
        greet(at(1, z, y), place == 0)
        for deep in far:
            greet(at(2, deep, y))
        greet(at(3, z, y))
        greet(at(3, z, other))

    loading[1].wait()
    high, low = halves(inverse[...])
    inverse_packed[:, :width] = high
    inverse_packed[:, width:] = low
    loading[0].wait()
    loading[2].wait()
    loading[3].wait()
    targets = [pattern[0, 0, block] for block in range(supers)]

    def block_for(target):
        found = jnp.int32(0)
        for block in range(supers):
            found = jnp.where(targets[block] == target, jnp.int32(block), found)
        return factor[found]

    def squared():
        return times(inverse[...].T, inverse_packed[...])

    @pl.when(place == 0)
    def _():
        free[0] = iter(range(count // 2))
        for block in range(supers):
            high, low = halves(block_for(block).T)
            turned[:width, block * width:(block + 1) * width] = high
            turned[width:, block * width:(block + 1) * width] = low
        fresh = times_transposed(rhs[...], inverse_packed[...])
        rhs[...] = fresh
        forward_ref[...] = fresh
        for piece in range(4):
            q, c = piece // 2, piece % 2
            part = slice(c * half + q * rows, c * half + (q + 1) * rows)
            wide = times_turned(rhs[part, :], turned[...])
            for deep in range(depth):
                for side in range(2):
                    block = 2 * deep + side
                    outbox[piece, deep, side] = wide[:, block * width:(block + 1) * width]
            if piece == 0:
                pl.semaphore_wait(barrier, 2 * supers - 1)
            if c == 0:
                inbox1[q, me] = outbox[piece, z]
            for deep in far:
                for side in (other, y):
                    remote(
                        lambda piece=piece, q=q, c=c, deep=deep, side=side: (
                            outbox.at[piece, deep], inbox1.at[q, me], sem1.at[q], at(c, deep, side)
                        ),
                        (lambda deep=deep: deep != z) if c == 0 and side is y else None,
                    )
        for block in range(supers):
            product = times(block_for(block), inverse_packed[...])
            high, low = halves(product)
            packed[block * width:(block + 1) * width, :width] = high
            packed[block * width:(block + 1) * width, width:] = low
        for deep in range(depth):
            arrive(near1.at[y, deep], near1_sem.at[y, deep])
        later[0] = take()

    @pl.when(place == 1)
    def _():
        free[0] = iter(range(count // 2))
        pl.semaphore_wait(barrier, 3)
        first, second = pl.ds(0, half), pl.ds(half, half)
        remote(lambda: (rhs.at[first], side1.at[y], side_sem.at[0], at(0, z, y)))
        remote(lambda: (rhs.at[first], side1.at[y], side_sem.at[0], at(0, z, other)))
        remote(lambda: (rhs.at[second], side1.at[y], side_sem.at[0], at(1, z, other)))
        side1[y] = rhs[second, :]
        for deep in range(depth):
            made[deep] = times(block_for(2 * deep + other), inverse_packed[...])
            remote(lambda deep=deep: (made.at[deep], near1.at[y, deep], near1_sem.at[y, deep], at(1, z, other)))
        for deep in range(depth):
            near1[y, deep] = times(block_for(2 * deep + y), inverse_packed[...])
            remote(lambda deep=deep: (near1.at[y, deep], near1.at[y, deep], near1_sem.at[y, deep], at(0, z, y)))
        square1[...] = squared()
        remote(lambda: (square1, square1, square_sem.at[0], at(0, z, y)))
        for deep in range(depth):
            arrive(near1.at[other, deep], near1_sem.at[other, deep])
            remote(lambda deep=deep: (near1.at[other, deep], near1.at[other, deep], near1_sem.at[other, deep], at(0, z, y)))
        later[1] = take()

    @pl.when(place == 2)
    def _():
        free[0] = iter(range(count // 2))
        for block in range(supers):
            made[block] = times(block_for(block), inverse_packed[...])
            if block == 0:
                pl.semaphore_wait(barrier, supers)
                for deep in far:
                    for c in range(2):
                        remote(lambda c=c, deep=deep: (rhs.at[pl.ds(c * half, half)], side2.at[z], side_sem.at[1], at(c, deep, y)))
            deep, side = block // 2, block % 2
            remote(lambda deep=deep, side=side, block=block: (made.at[block], near2.at[z, side], near2_sem.at[z, side], at(side, deep, y)))
        square2[...] = squared()
        for c in range(2):
            remote(lambda c=c: (square2, square2, square_sem.at[1], at(c, z, y)))
        finish(take())

    @pl.when(place == 3)
    def _():
        free[0] = iter(range(count // 2))
        square3[y] = squared()
        pl.semaphore_wait(barrier, 4)
        for c in range(2):
            for side in (other, y):
                remote(lambda c=c, side=side: (rhs.at[pl.ds(c * half, half)], side3.at[y], side_sem.at[2], at(c, z, side)))
                remote(lambda c=c, side=side: (square3.at[y], square3.at[y], square_sem.at[2], at(c, z, side)))
        finish(take())

    @pl.when(place < 2)
    def _():
        free[0] = iter(range(count // 2, count))
        @pl.when(place == 0)
        def _():
            for deep in range(depth):
                arrive(near1.at[other, deep], near1_sem.at[other, deep])

        for side in range(2):
            for deep in range(depth):
                value = near1[side, deep]
                pack_into(turned1, side, deep, depth, value.T)
                pack_into(packed1, deep, side, 2, value)

        @pl.when(place == 0)
        def _():
            arrive(side1, side_sem.at[0])
            arrive(square1, square_sem.at[0])

        @pl.when(place == 1)
        def _():
            arrive(side1.at[0], side_sem.at[0])

        pack_into(mean1, 0, 0, 1, square1[...])

        for q in range(2):
            part = slice(q * rows, (q + 1) * rows)

            @pl.when(place == 0)
            def _():
                arrive(inbox1.at[q, pl.ds(0, supers - 1)], sem1.at[q])

            @pl.when(place == 1)
            def _():
                arrive(inbox1.at[q], sem1.at[q])

            for side in range(2):
                held1[q, side] = side1[side, part, :] - jnp.sum(inbox1[q, :, side], axis=0)
            wide = times(jnp.concatenate([held1[q, 0], held1[q, 1]], axis=1), turned1[...])
            for deep in range(depth):
                inbox2[q, z, deep] = wide[:, deep * width:(deep + 1) * width]
            for deep in far[:-1]:
                remote(lambda q=q, deep=deep: (inbox2.at[q, z], inbox2.at[q, z], sem2.at[q], at(place, deep, y)))
            kept1[q] = times(held1[q, y], mean1[...])
            remote(lambda q=q: (held1.at[q, y], back_u.at[2 * q], back_sem.at[0, q], at(1, z, y)), lambda: place == 0)

            @pl.when(place == 1)
            def _():
                back_u[2 * q + 1] = held1[q, y]

        for deep in range(depth):
            arrive(near2.at[deep, place], near2_sem.at[deep, place])
            remote(lambda deep=deep: (near2.at[deep, place], near2.at[deep, place], near2_sem.at[deep, place], at(1 - place, z, y)))
        arrive(side2, side_sem.at[1])
        arrive(square2, square_sem.at[1])
        pack_into(mean2, 0, 0, 1, square2[...])
        arrive(side3, side_sem.at[2])
        arrive(square3, square_sem.at[2])
        for side in range(2):
            pack_into(mean3, side, 0, 1, square3[side])
        for deep in range(depth):
            arrive(near2.at[deep, 1 - place], near2_sem.at[deep, 1 - place])
        for deep in range(depth):
            for side in range(2):
                value = near2[deep, side]
                pack_into(turned2, deep, side, 2, value.T)
                pack_into(packed2, side, deep, depth, value)

        for q in range(2):
            part = slice(q * rows, (q + 1) * rows)
            arrive(inbox2.at[q, pl.ds(0, depth - 1)], sem2.at[q])
            for deep in range(depth):
                held2[q, deep] = side2[deep, part, :] - jnp.sum(inbox2[q, :, deep], axis=0)
            wide = times(jnp.concatenate([held2[q, deep] for deep in range(depth)], axis=1), turned2[...])
            for side in range(2):
                inbox3[q, y, side] = wide[:, side * width:(side + 1) * width]
            remote(lambda q=q: (inbox3.at[q, y], inbox3.at[q, y], sem3.at[q], at(place, z, other)))
            kept2[q] = times(held2[q, z], mean2[...])
            remote(lambda q=q: (held2.at[q, z], back_u.at[2 * q + place], back_sem.at[0, 2 * q + place], at(2, z, y)))

        for q in range(2):
            part = slice(q * rows, (q + 1) * rows)
            arrive(inbox3.at[q, 0], sem3.at[q])
            fresh = []
            for side in range(2):
                held3[q, side] = side3[side, part, :] - inbox3[q, 0, side] - inbox3[q, 1, side]
                value = times(held3[q, side], mean3[side * width:(side + 1) * width, :])
                solved3[q, side] = value
                fresh.append(value)
            wide = times(jnp.concatenate(fresh, axis=1), packed2[...])
            for deep in range(depth):
                inbox4[q, z, deep] = -wide[:, deep * width:(deep + 1) * width]
            inbox4[q, z, z] = inbox4[q, z, z] + kept2[q]
            for deep in far[:-1]:
                remote(lambda q=q, deep=deep: (inbox4.at[q, z], inbox4.at[q, z], sem4.at[q], at(place, deep, y)))
            remote(lambda q=q: (held3.at[q, y], back_u.at[2 * q + place], back_sem.at[0, 2 * q + place], at(3, z, y)))
            remote(lambda q=q: (solved3.at[q, y], back_x.at[2 * q + place], back_sem.at[1, 2 * q + place], at(3, z, y)))

        for q in range(2):
            piece = 2 * q + place
            arrive(inbox4.at[q, pl.ds(0, depth - 1)], sem4.at[q])
            for deep in range(depth):
                solved2[q, deep] = jnp.sum(inbox4[q, :, deep], axis=0)
            wide = times(jnp.concatenate([solved2[q, deep] for deep in range(depth)], axis=1), packed1[...])
            for side in range(2):
                inbox5[piece, me, side] = -wide[:, side * width:(side + 1) * width]
            inbox5[piece, me, y] = inbox5[piece, me, y] + kept1[q]
            for deep in far:
                for side in (other, y):
                    remote(
                        lambda q=q, deep=deep, side=side: (
                            inbox5.at[2 * q + place, me], inbox5.at[2 * q + place, me],
                            sem5.at[2 * q + place], at(0, deep, side)
                        ),
                        (lambda deep=deep: (deep != z) | (place != 0)) if side is y else None,
                    )
            remote(lambda q=q: (inbox5.at[2 * q + place, me, other], back_pair.at[2 * q + place, y], back_sem.at[1, 2 * q + place], at(1, z, other)))
            remote(lambda q=q: (inbox5.at[2 * q + place, me, y], back_pair.at[2 * q + place, y], back_sem.at[1, 2 * q + place], at(1, z, y)), lambda: place == 0)

            @pl.when(place == 1)
            def _():
                back_pair[piece, y] = inbox5[piece, me, y]

            remote(lambda q=q: (solved2.at[q, z], back_x.at[2 * q + place], back_sem.at[1, 2 * q + place], at(2, z, y)))

        @pl.when(place == 0)
        def _():
            rhs[...] = times(forward_ref[...], inverse_packed[...])
            for piece in range(4):
                q, c = piece // 2, piece % 2
                part = slice(c * half + q * rows, c * half + (q + 1) * rows)
                arrive(inbox5.at[piece, pl.ds(0, supers - 1 + c)], sem5.at[piece])
                chosen = []
                for deep in range(depth):
                    for side in range(2):
                        chosen.append(inbox5[piece, 2 * deep, side] + inbox5[piece, 2 * deep + 1, side])
                answer_ref[part, :] = rhs[part, :] - times(jnp.concatenate(chosen, axis=1), packed[...])

        finish(take())

    for index in range(2):
        @pl.when(place == index)
        def _():
            finish(later[index])

    @pl.when(place > 0)
    def _():
        for piece in range(4):
            q, c = piece // 2, piece % 2
            part = slice(c * half + q * rows, c * half + (q + 1) * rows)
            if c == 0:
                @pl.when(place == 1)
                def _():
                    arrive(back_u.at[piece], back_sem.at[0, q])

            @pl.when(place > 1)
            def _():
                arrive(back_u.at[piece], back_sem.at[0, piece])

            rhs[part, :] = back_u[piece]
        forward_ref[...] = times_transposed(rhs[...], inverse_packed[...])
        for piece in range(4):
            q, c = piece // 2, piece % 2
            part = slice(c * half + q * rows, c * half + (q + 1) * rows)

            @pl.when(place == 1)
            def _():
                arrive(back_pair.at[piece, pl.ds(0, 2 - c)], back_sem.at[1, piece])
                answer_ref[part, :] = back_pair[piece, 0] + back_pair[piece, 1]

            @pl.when(place > 1)
            def _():
                arrive(back_x.at[piece], back_sem.at[1, piece])
                answer_ref[part, :] = back_x[piece]


def spread_body(rhs, inverse, factor, pattern):
    supers = lax.axis_size("col")
    loads, width = rhs.shape[2:]
    depth = supers // 2
    rows, half = loads // 4, loads // 2
    f32, bf16 = jnp.float32, jnp.bfloat16
    square = (width, width)
    piece = (rows, width)
    anywhere = pl.BlockSpec(memory_space=pl.ANY)
    dma = pltpu.SemaphoreType.DMA
    both = pl.pallas_call(
        functools.partial(spread_kernel, supers),
        out_shape=pltpu.VMEM((2, loads, width), f32),
        in_specs=[anywhere] * 4,
        out_specs=pl.BlockSpec(memory_space=pltpu.VMEM),
        scratch_shapes=[
            pltpu.VMEM((loads, width), f32),
            pltpu.VMEM(square, f32),
            pltpu.VMEM((supers,) + square, f32),
            pltpu.SMEM((1, 1, supers), jnp.int32),
            pltpu.VMEM((width, 2 * width), bf16),
            pltpu.VMEM((supers * width, 2 * width), bf16),
            pltpu.VMEM((2 * width, supers * width), bf16),
            pltpu.VMEM((supers,) + square, f32),
            pltpu.VMEM((2, depth) + square, f32),
            pltpu.VMEM((depth, 2) + square, f32),
            pltpu.VMEM(square, f32),
            pltpu.VMEM(square, f32),
            pltpu.VMEM((2,) + square, f32),
            pltpu.VMEM((2, half, width), f32),
            pltpu.VMEM((depth, half, width), f32),
            pltpu.VMEM((2, half, width), f32),
            pltpu.VMEM((2 * width, 2 * depth * width), bf16),
            pltpu.VMEM((depth * width, 4 * width), bf16),
            pltpu.VMEM((depth * width, 4 * width), bf16),
            pltpu.VMEM((2 * width, 2 * depth * width), bf16),
            pltpu.VMEM((width, 2 * width), bf16),
            pltpu.VMEM((width, 2 * width), bf16),
            pltpu.VMEM((2 * width, 2 * width), bf16),
            pltpu.VMEM((4, depth, 2) + piece, f32),
            pltpu.VMEM((2, supers, 2) + piece, f32),
            pltpu.VMEM((2, depth, depth) + piece, f32),
            pltpu.VMEM((2, 2, 2) + piece, f32),
            pltpu.VMEM((2, depth, depth) + piece, f32),
            pltpu.VMEM((4, supers, 2) + piece, f32),
            pltpu.VMEM((2, 2) + piece, f32),
            pltpu.VMEM((2, depth) + piece, f32),
            pltpu.VMEM((2, 2) + piece, f32),
            pltpu.VMEM((2,) + piece, f32),
            pltpu.VMEM((2,) + piece, f32),
            pltpu.VMEM((2, depth) + piece, f32),
            pltpu.VMEM((2, 2) + piece, f32),
            pltpu.VMEM((4,) + piece, f32),
            pltpu.VMEM((4,) + piece, f32),
            pltpu.VMEM((4, 2) + piece, f32),
            dma((4,)),
            dma((160,)),
            dma((2, depth)),
            dma((depth, 2)),
            dma((3,)),
            dma((3,)),
            dma((2,)),
            dma((2,)),
            dma((2,)),
            dma((2,)),
            dma((4,)),
            dma((2, 4)),
        ],
        compiler_params=pltpu.CompilerParams(collective_id=0, has_side_effects=True),
    )(rhs[0, 0], inverse[0, 0], factor[0, 0], pattern)
    return (both[None, :1], both[None, 1:])


def solution(mesh):
    levels, supers = mesh.shape["chain"], mesh.shape["col"]

    def chosen(rhs, inverse, factor, pattern):
        dense = levels == 4 and factor.shape[2] == supers and supers % 4 == 0 and rhs.shape[2] % 32 == 0
        return (spread_body if dense else body)(rhs, inverse, factor, pattern)

    in_specs = (
        P("chain", "col", None, None),
        P("chain", "col", None, None),
        P("chain", "col", None, None, None),
        P("chain", "col", None),
    )
    out_specs = (P("chain", "col", None, None), P("chain", "col", None, None))
    return jax.shard_map(chosen, mesh=mesh, in_specs=in_specs, out_specs=out_specs, check_vma=False)
```

```python
import functools

import jax
import jax.numpy as jnp
from jax import lax
from jax.experimental import pallas as pl
from jax.experimental.pallas import tpu as pltpu
from jax.sharding import PartitionSpec as P

PIECES = 4
MESH = pl.DeviceIdType.MESH


def halves(value):
    high = value.astype(jnp.bfloat16)
    low = (value - high.astype(jnp.float32)).astype(jnp.bfloat16)
    return high, low


def times_transposed(value, packed):
    rows = value.shape[0]
    high, low = halves(value)
    stacked = jnp.concatenate(
        [jnp.concatenate([high, low], axis=1), jnp.concatenate([low, high], axis=1)], axis=0
    )
    both = lax.dot_general(
        stacked, packed, (((1,), (1,)), ((), ())), preferred_element_type=jnp.float32
    )
    return both[:rows] + both[rows:]


def times_turned(value, turned):
    rows = value.shape[0]
    high, low = halves(value)
    stacked = jnp.concatenate(
        [jnp.concatenate([high, low], axis=1), jnp.concatenate([low, high], axis=1)], axis=0
    )
    both = jnp.dot(stacked, turned, preferred_element_type=jnp.float32)
    return both[:rows] + both[rows:]


def times(value, packed):
    rows = value.shape[0]
    width = packed.shape[1] // 2
    high, low = halves(value)
    both = jnp.dot(
        jnp.concatenate([high, low], axis=0), packed, preferred_element_type=jnp.float32
    )
    summed = both[:rows] + both[rows:]
    return summed[:, :width] + summed[:, width:]


def kernel(
    levels, supers, rhs_hbm, inverse_hbm, factor_hbm, pattern_hbm, both_ref,
    rhs, inverse, factor, pattern, inverse_packed, packed, turned, terms, outbox, inbox, solved,
    load_sem, outbox_sem, inbox_sem, solved_sem, arrived_sem, *arrived,
):
    forward_ref, answer_ref = both_ref.at[0], both_ref.at[1]
    place = lax.axis_index("chain")
    me = lax.axis_index("col")
    count, _, width = factor.shape
    loads = rhs.shape[0]
    rows = loads // PIECES
    loading = [
        pltpu.make_async_copy(source, target, load_sem.at[at])
        for at, (source, target) in enumerate(
            ((rhs_hbm, rhs), (inverse_hbm, inverse), (factor_hbm, factor), (pattern_hbm, pattern))
        )
    ]
    for copy in loading:
        copy.start()
    peers = [lax.rem(me + shift, supers) for shift in range(supers)]
    upper = lax.div(2 * me, supers)
    distant = [(1 - upper) * (supers - 1 - k) + upper * k for k in range(supers)]
    distant = [(peer, lax.rem(peer - me + supers, supers)) for peer in distant]

    barrier = pltpu.get_barrier_semaphore()

    @pl.when(place > 0)
    def _():
        for peer in peers:
            pl.semaphore_signal(
                barrier, inc=1, device_id={"chain": place - 1, "col": peer}, device_id_type=MESH
            )

    @pl.when(place < levels - 1)
    def _():
        for peer in peers:
            pl.semaphore_signal(
                barrier, inc=1, device_id={"chain": place + 1, "col": peer}, device_id_type=MESH
            )

    loading[0].wait()
    loading[1].wait()
    high, low = halves(inverse[...])
    inverse_packed[:, :width] = high
    inverse_packed[:, width:] = low

    full = count == supers

    def pack(block, value):
        high, low = halves(value)
        packed[block * width:(block + 1) * width, :width] = high
        packed[block * width:(block + 1) * width, width:] = low

    def pack_turned(block, value):
        high, low = halves(value.T)
        turned[:width, block * width:(block + 1) * width] = high
        turned[width:, block * width:(block + 1) * width] = low

    def block_of(block):
        return factor[jnp.maximum(origin[block], 0)] if full else factor[block]

    loading[2].wait()
    loading[3].wait()
    targets = [pattern[0, 0, block] for block in range(count)]
    origin = []
    for peer in peers:
        at = jnp.int32(-1)
        for block in range(count):
            at = jnp.where(targets[block] == peer, jnp.int32(block), at)
        origin.append(at)
    slots = [lax.rem(me - target + supers, supers) for target in targets]

    @pl.when(place == 0)
    def _():
        for block in range(count):
            pack_turned(block, block_of(block))
        rhs[...] = times_transposed(rhs[...], inverse_packed[...])
        forward_ref[...] = rhs[...]

    @pl.when((place > 0) & (place < levels - 1))
    def _():
        for block in range(count):
            product = times(block_of(block), inverse_packed[...])
            pack(block, product)
            pack_turned(block, product)

    @pl.when(place == levels - 1)
    def _():
        pack(0, times(inverse[...].T, inverse_packed[...]))

    def term_copy(piece, peer, shift):
        return pltpu.make_async_remote_copy(
            src_ref=outbox.at[piece, shift],
            dst_ref=inbox.at[piece, shift],
            send_sem=outbox_sem.at[piece, shift],
            recv_sem=inbox_sem.at[piece],
            device_id={"chain": place + 1, "col": peer},
            device_id_type=MESH,
        )

    def answer_copy(piece, peer, shift):
        return pltpu.make_async_remote_copy(
            src_ref=solved.at[piece],
            dst_ref=arrived[piece].at[shift],
            send_sem=solved_sem.at[piece, shift],
            recv_sem=arrived_sem.at[piece],
            device_id={"chain": place - 1, "col": peer},
            device_id_type=MESH,
        )

    for piece in range(PIECES):
        part = pl.ds(piece * rows, rows)

        @pl.when(place > 0)
        def _():
            pltpu.make_async_copy(inbox.at[piece], inbox.at[piece], inbox_sem.at[piece]).wait()
            total = rhs[part, :] - jnp.sum(inbox[piece], axis=0)
            rhs[part, :] = total

        @pl.when(place < levels - 1)
        def _():
            wide = times_turned(rhs[part, :], turned[...])
            if full:
                for shift in range(supers):
                    outbox[piece, shift] = wide[:, shift * width:(shift + 1) * width]
            else:
                for block in range(count):
                    terms[block] = wide[:, block * width:(block + 1) * width]
                for shift in range(supers):
                    picked = terms[jnp.maximum(origin[shift], 0)]
                    outbox[piece, shift] = jnp.where(origin[shift] >= 0, picked, 0.0)

        @pl.when(place == levels - 1)
        def _():
            fresh = times(rhs[part, :], packed[:width, :])
            solved[piece] = fresh
            answer_ref[part, :] = fresh

        if piece == 0:
            pl.semaphore_wait(
                barrier, jnp.where(place > 0, supers, 0) + jnp.where(place < levels - 1, supers, 0)
            )

        @pl.when(place < levels - 1)
        def _():
            for peer, shift in distant:
                term_copy(piece, peer, shift).start()

        @pl.when(place == levels - 1)
        def _():
            for peer, shift in distant:
                answer_copy(piece, peer, shift).start()

    @pl.when(place > 0)
    def _():
        forward_ref[...] = times_transposed(rhs[...], inverse_packed[...])

    @pl.when(place == 0)
    def _():
        for block in range(count):
            pack(block, times(block_of(block), inverse_packed[...]))

    @pl.when(place < levels - 1)
    def _():
        rhs[...] = times(forward_ref[...], inverse_packed[...])
        for piece in range(PIECES):
            part = pl.ds(piece * rows, rows)
            pltpu.make_async_copy(arrived[piece], arrived[piece], arrived_sem.at[piece]).wait()
            if full:
                chosen = [arrived[piece][(supers - shift) % supers] for shift in range(supers)]
            else:
                chosen = [arrived[piece][slot] for slot in slots]
            picked = jnp.concatenate(chosen, axis=1)
            fresh = rhs[part, :] - times(picked, packed[...])
            solved[piece] = fresh
            answer_ref[part, :] = fresh

            @pl.when(place > 0)
            def _():
                for peer, shift in distant:
                    answer_copy(piece, peer, shift).start()

    @pl.when(place < levels - 1)
    def _():
        for piece in range(PIECES):
            for peer, shift in distant:
                term_copy(piece, peer, shift).wait_send()

    @pl.when(place > 0)
    def _():
        for piece in range(PIECES):
            for peer, shift in distant:
                answer_copy(piece, peer, shift).wait_send()


def body(rhs, inverse, factor, pattern):
    levels = lax.axis_size("chain")
    supers = lax.axis_size("col")
    loads, width = rhs.shape[2:]
    count = factor.shape[2]
    rows = loads // PIECES
    block = pltpu.VMEM((2, loads, width), jnp.float32)
    anywhere = pl.BlockSpec(memory_space=pl.ANY)
    both = pl.pallas_call(
        functools.partial(kernel, levels, supers),
        out_shape=block,
        in_specs=[anywhere] * 4,
        out_specs=pl.BlockSpec(memory_space=pltpu.VMEM),
        scratch_shapes=[
            pltpu.VMEM((loads, width), jnp.float32),
            pltpu.VMEM((width, width), jnp.float32),
            pltpu.VMEM((count, width, width), jnp.float32),
            pltpu.SMEM((1, 1, count), jnp.int32),
            pltpu.VMEM((width, 2 * width), jnp.bfloat16),
            pltpu.VMEM((count * width, 2 * width), jnp.bfloat16),
            pltpu.VMEM((2 * width, count * width), jnp.bfloat16),
            pltpu.VMEM((count, rows, width), jnp.float32),
            pltpu.VMEM((PIECES, supers, rows, width), jnp.float32),
            pltpu.VMEM((PIECES, supers, rows, width), jnp.float32),
            pltpu.VMEM((PIECES, rows, width), jnp.float32),
            pltpu.SemaphoreType.DMA((4,)),
            pltpu.SemaphoreType.DMA((PIECES, supers)),
            pltpu.SemaphoreType.DMA((PIECES,)),
            pltpu.SemaphoreType.DMA((PIECES, supers)),
            pltpu.SemaphoreType.DMA((PIECES,)),
            *[pltpu.VMEM((supers, rows, width), jnp.float32)] * PIECES,
        ],
        compiler_params=pltpu.CompilerParams(collective_id=0, has_side_effects=True),
    )(rhs[0, 0], inverse[0, 0], factor[0, 0], pattern)
    return (both[None, :1], both[None, 1:])


def solution(mesh):
    in_specs = (
        P("chain", "col", None, None),
        P("chain", "col", None, None),
        P("chain", "col", None, None, None),
        P("chain", "col", None),
    )
    out_specs = (P("chain", "col", None, None), P("chain", "col", None, None))
    return jax.shard_map(body, mesh=mesh, in_specs=in_specs, out_specs=out_specs, check_vma=False)
```

```python
import functools

import jax
import jax.numpy as jnp
from jax import lax
from jax.experimental import pallas as pl
from jax.experimental.pallas import tpu as pltpu
from jax.sharding import PartitionSpec as P

PIECES = 4
MESH = pl.DeviceIdType.MESH


def halves(value):
    high = value.astype(jnp.bfloat16)
    low = (value - high.astype(jnp.float32)).astype(jnp.bfloat16)
    return high, low


def times_transposed(value, packed):
    rows = value.shape[0]
    high, low = halves(value)
    stacked = jnp.concatenate(
        [jnp.concatenate([high, low], axis=1), jnp.concatenate([low, high], axis=1)], axis=0
    )
    both = lax.dot_general(
        stacked, packed, (((1,), (1,)), ((), ())), preferred_element_type=jnp.float32
    )
    return both[:rows] + both[rows:]


def times_turned(value, turned):
    rows = value.shape[0]
    high, low = halves(value)
    stacked = jnp.concatenate(
        [jnp.concatenate([high, low], axis=1), jnp.concatenate([low, high], axis=1)], axis=0
    )
    both = jnp.dot(stacked, turned, preferred_element_type=jnp.float32)
    return both[:rows] + both[rows:]


def times(value, packed):
    rows = value.shape[0]
    width = packed.shape[1] // 2
    high, low = halves(value)
    both = jnp.dot(
        jnp.concatenate([high, low], axis=0), packed, preferred_element_type=jnp.float32
    )
    summed = both[:rows] + both[rows:]
    return summed[:, :width] + summed[:, width:]


def kernel(
    levels, supers, rhs_hbm, inverse_hbm, factor_hbm, pattern_hbm, both_ref,
    rhs, inverse, factor, pattern, inverse_packed, packed, turned, terms, outbox, inbox, solved,
    load_sem, outbox_sem, inbox_sem, solved_sem, arrived_sem, *arrived,
):
    forward_ref, answer_ref = both_ref.at[0], both_ref.at[1]
    place = lax.axis_index("chain")
    me = lax.axis_index("col")
    count, _, width = factor.shape
    loads = rhs.shape[0]
    rows = loads // PIECES
    loading = [
        pltpu.make_async_copy(source, target, load_sem.at[at])
        for at, (source, target) in enumerate(
            ((rhs_hbm, rhs), (inverse_hbm, inverse), (factor_hbm, factor), (pattern_hbm, pattern))
        )
    ]
    for copy in loading:
        copy.start()
    peers = [lax.rem(me + shift, supers) for shift in range(supers)]
    upper = lax.div(2 * me, supers)
    distant = [(1 - upper) * (supers - 1 - k) + upper * k for k in range(supers)]
    distant = [(peer, lax.rem(peer - me + supers, supers)) for peer in distant]

    barrier = pltpu.get_barrier_semaphore()

    @pl.when(place > 0)
    def _():
        for peer in peers:
            pl.semaphore_signal(
                barrier, inc=1, device_id={"chain": place - 1, "col": peer}, device_id_type=MESH
            )

    @pl.when(place < levels - 1)
    def _():
        for peer in peers:
            pl.semaphore_signal(
                barrier, inc=1, device_id={"chain": place + 1, "col": peer}, device_id_type=MESH
            )

    loading[0].wait()
    loading[1].wait()
    high, low = halves(inverse[...])
    inverse_packed[:, :width] = high
    inverse_packed[:, width:] = low

    full = count == supers

    def pack(block, value):
        high, low = halves(value)
        packed[block * width:(block + 1) * width, :width] = high
        packed[block * width:(block + 1) * width, width:] = low

    def pack_turned(block, value):
        high, low = halves(value.T)
        turned[:width, block * width:(block + 1) * width] = high
        turned[width:, block * width:(block + 1) * width] = low

    def block_of(block):
        return factor[jnp.maximum(origin[block], 0)] if full else factor[block]

    loading[2].wait()
    loading[3].wait()
    targets = [pattern[0, 0, block] for block in range(count)]
    origin = []
    for peer in peers:
        at = jnp.int32(-1)
        for block in range(count):
            at = jnp.where(targets[block] == peer, jnp.int32(block), at)
        origin.append(at)
    slots = [lax.rem(me - target + supers, supers) for target in targets]

    @pl.when(place == 0)
    def _():
        for block in range(count):
            pack_turned(block, block_of(block))
        rhs[...] = times_transposed(rhs[...], inverse_packed[...])
        forward_ref[...] = rhs[...]

    @pl.when((place > 0) & (place < levels - 1))
    def _():
        for block in range(count):
            product = times(block_of(block), inverse_packed[...])
            pack(block, product)
            pack_turned(block, product)

    @pl.when(place == levels - 1)
    def _():
        pack(0, times(inverse[...].T, inverse_packed[...]))

    def term_copy(piece, peer, shift):
        return pltpu.make_async_remote_copy(
            src_ref=outbox.at[piece, shift],
            dst_ref=inbox.at[piece, shift],
            send_sem=outbox_sem.at[piece, shift],
            recv_sem=inbox_sem.at[piece],
            device_id={"chain": place + 1, "col": peer},
            device_id_type=MESH,
        )

    def answer_copy(piece, peer, shift):
        return pltpu.make_async_remote_copy(
            src_ref=solved.at[piece],
            dst_ref=arrived[piece].at[shift],
            send_sem=solved_sem.at[piece, shift],
            recv_sem=arrived_sem.at[piece],
            device_id={"chain": place - 1, "col": peer},
            device_id_type=MESH,
        )

    for piece in range(PIECES):
        part = pl.ds(piece * rows, rows)

        @pl.when(place > 0)
        def _():
            pltpu.make_async_copy(inbox.at[piece], inbox.at[piece], inbox_sem.at[piece]).wait()
            total = rhs[part, :] - jnp.sum(inbox[piece], axis=0)
            rhs[part, :] = total

        @pl.when(place < levels - 1)
        def _():
            wide = times_turned(rhs[part, :], turned[...])
            if full:
                for shift in range(supers):
                    outbox[piece, shift] = wide[:, shift * width:(shift + 1) * width]
            else:
                for block in range(count):
                    terms[block] = wide[:, block * width:(block + 1) * width]
                for shift in range(supers):
                    picked = terms[jnp.maximum(origin[shift], 0)]
                    outbox[piece, shift] = jnp.where(origin[shift] >= 0, picked, 0.0)

        @pl.when(place == levels - 1)
        def _():
            fresh = times(rhs[part, :], packed[:width, :])
            solved[piece] = fresh
            answer_ref[part, :] = fresh

        if piece == 0:
            pl.semaphore_wait(
                barrier, jnp.where(place > 0, supers, 0) + jnp.where(place < levels - 1, supers, 0)
            )

        @pl.when(place < levels - 1)
        def _():
            for peer, shift in distant:
                term_copy(piece, peer, shift).start()

        @pl.when(place == levels - 1)
        def _():
            for peer, shift in distant:
                answer_copy(piece, peer, shift).start()

    @pl.when(place > 0)
    def _():
        forward_ref[...] = times_transposed(rhs[...], inverse_packed[...])

    @pl.when(place == 0)
    def _():
        for block in range(count):
            pack(block, times(block_of(block), inverse_packed[...]))

    @pl.when(place < levels - 1)
    def _():
        rhs[...] = times(forward_ref[...], inverse_packed[...])
        for piece in range(PIECES):
            part = pl.ds(piece * rows, rows)
            pltpu.make_async_copy(arrived[piece], arrived[piece], arrived_sem.at[piece]).wait()
            if full:
                chosen = [arrived[piece][(supers - shift) % supers] for shift in range(supers)]
            else:
                chosen = [arrived[piece][slot] for slot in slots]
            picked = jnp.concatenate(chosen, axis=1)
            fresh = rhs[part, :] - times(picked, packed[...])
            solved[piece] = fresh
            answer_ref[part, :] = fresh

            @pl.when(place > 0)
            def _():
                for peer, shift in distant:
                    answer_copy(piece, peer, shift).start()

    @pl.when(place < levels - 1)
    def _():
        for piece in range(PIECES):
            for peer, shift in distant:
                term_copy(piece, peer, shift).wait_send()

    @pl.when(place > 0)
    def _():
        for piece in range(PIECES):
            for peer, shift in distant:
                answer_copy(piece, peer, shift).wait_send()


def body(rhs, inverse, factor, pattern):
    levels = lax.axis_size("chain")
    supers = lax.axis_size("col")
    loads, width = rhs.shape[2:]
    count = factor.shape[2]
    rows = loads // PIECES
    block = pltpu.VMEM((2, loads, width), jnp.float32)
    anywhere = pl.BlockSpec(memory_space=pl.ANY)
    both = pl.pallas_call(
        functools.partial(kernel, levels, supers),
        out_shape=block,
        in_specs=[anywhere] * 4,
        out_specs=pl.BlockSpec(memory_space=pltpu.VMEM),
        scratch_shapes=[
            pltpu.VMEM((loads, width), jnp.float32),
            pltpu.VMEM((width, width), jnp.float32),
            pltpu.VMEM((count, width, width), jnp.float32),
            pltpu.SMEM((1, 1, count), jnp.int32),
            pltpu.VMEM((width, 2 * width), jnp.bfloat16),
            pltpu.VMEM((count * width, 2 * width), jnp.bfloat16),
            pltpu.VMEM((2 * width, count * width), jnp.bfloat16),
            pltpu.VMEM((count, rows, width), jnp.float32),
            pltpu.VMEM((PIECES, supers, rows, width), jnp.float32),
            pltpu.VMEM((PIECES, supers, rows, width), jnp.float32),
            pltpu.VMEM((PIECES, rows, width), jnp.float32),
            pltpu.SemaphoreType.DMA((4,)),
            pltpu.SemaphoreType.DMA((PIECES, supers)),
            pltpu.SemaphoreType.DMA((PIECES,)),
            pltpu.SemaphoreType.DMA((PIECES, supers)),
            pltpu.SemaphoreType.DMA((PIECES,)),
            *[pltpu.VMEM((supers, rows, width), jnp.float32)] * PIECES,
        ],
        compiler_params=pltpu.CompilerParams(collective_id=0, has_side_effects=True),
    )(rhs[0, 0], inverse[0, 0], factor[0, 0], pattern)
    return (both[None, :1], both[None, 1:])


def folded_kernel(
    levels, supers, rhs_hbm, inverse_hbm, factor_hbm, pattern_hbm, both_ref,
    rhs, inverse, factor, pattern, inverse_packed, packed, turned, square, made,
    outbox, inbox, inbox_top, arrived, arrived_top, solved, yout, back,
    load_sem, send_sem, inbox_sem, top_sem, arrived_sem, back_top_sem, extra_sem, made_sem, back_sem,
):
    forward_ref, answer_ref = both_ref.at[0], both_ref.at[1]
    place = lax.axis_index("chain")
    me = lax.axis_index("col")
    width = factor.shape[1]
    rows = rhs.shape[1] // PIECES
    below, top = levels - 2, levels - 1
    depth = supers // 2
    quarter = depth // 4
    z, y = lax.div(me, 2), lax.rem(me, 2)
    upper = lax.div(z, depth // 2)
    middle = lax.rem(lax.div(lax.div(z, quarter) + 1, 2), 2)
    mate = 2 * (z + (1 - 2 * middle) * quarter * (1 - 2 * upper)) + y
    mate_chain = below + top - place
    slot = lax.div(place, top)
    first_id = me + (place - below) * (mate - me)
    second_id = me + (top - place) * (mate - me)
    works = (place >= below) & (middle == 1)
    lends = (place >= below) & (middle == 0)
    count = send_sem.shape[0]
    sends = []
    free = [None]
    lent = []

    def host(level, index):
        deep, side = index // 2, index % 2
        if level < below or quarter <= deep < 3 * quarter:
            return level, index
        deep += quarter if deep < quarter else -quarter
        return below + top - level, 2 * deep + side

    hosts = sorted({host(level, index) for level in (below, top) for index in range(supers)})

    def away(device):
        return (place != device[0]) | (me != device[1])

    def copy_of(build, index):
        source, target, arrival, device = build()
        return pltpu.make_async_remote_copy(
            src_ref=source, dst_ref=target, send_sem=send_sem.at[index], recv_sem=arrival,
            device_id={"chain": device[0], "col": device[1]}, device_id_type=MESH,
        )

    def remote(build):
        index = next(free[0])
        copy_of(build, index).start()
        sends.append((build, index, None))

    def scatter(build, reached):
        indices = [next(free[0]) for _ in range(supers)]

        def start(item):
            if reached(item) is None:
                copy_of(lambda: build(item), indices[item]).start()
            else:
                pl.when(away(reached(item)))(lambda: copy_of(lambda: build(item), indices[item]).start())

        for side in range(2):
            @pl.when(upper == side)
            def _():
                for item in (range(supers) if side else reversed(range(supers))):
                    start(item)

        for item in range(supers):
            sends.append((lambda item=item: build(item), indices[item], reached(item)))

    def finish():
        for build, index, device in sends:
            if device is None:
                copy_of(build, index).wait_send()
            else:
                pl.when(away(device))(lambda build=build, index=index: copy_of(build, index).wait_send())
        sends.clear()

    def arrive(ref, sem):
        pltpu.make_async_copy(ref, ref, sem).wait()

    def begin():
        free[0] = iter(range(count))

    def pack(block, value):
        high, low = halves(value)
        packed[block * width:(block + 1) * width, :width] = high
        packed[block * width:(block + 1) * width, width:] = low

    def pack_turned(block, value):
        high, low = halves(value.T)
        turned[:width, block * width:(block + 1) * width] = high
        turned[width:, block * width:(block + 1) * width] = low

    def pack_inverse(which):
        high, low = halves(inverse[which])
        inverse_packed[which, :, :width] = high
        inverse_packed[which, :, width:] = low

    loading = [
        pltpu.make_async_copy(source, target, load_sem.at[at])
        for at, (source, target) in enumerate(
            (
                (rhs_hbm, rhs.at[slot]), (inverse_hbm, inverse.at[slot]),
                (factor_hbm, factor), (pattern_hbm, pattern),
            )
        )
    ]
    for copy in loading:
        copy.start()

    barrier = pltpu.get_barrier_semaphore()

    def greet(chain, col):
        pl.semaphore_signal(
            barrier, inc=1, device_id={"chain": chain, "col": col}, device_id_type=MESH
        )

    peers = [lax.rem(me + shift, supers) for shift in range(supers)]

    @pl.when((place > 0) & (place < below))
    def _():
        for peer in peers:
            greet(place - 1, peer)

    @pl.when(works)
    def _():
        greet(mate_chain, mate)
        for peer in peers:
            greet(below - 1, peer)
        for chain, col in hosts:
            pl.when(away((chain, col)))(lambda chain=chain, col=col: greet(chain, col))

    @pl.when(lends)
    def _():
        begin()
        pl.semaphore_wait(barrier, 1)
        remote(lambda: (rhs_hbm, rhs.at[slot], extra_sem.at[0], (mate_chain, mate)))
        remote(lambda: (inverse_hbm, inverse.at[slot], extra_sem.at[1], (mate_chain, mate)))
        lent.extend(sends)
        sends.clear()

    loading[0].wait()
    loading[1].wait()
    pack_inverse(slot)
    loading[2].wait()
    loading[3].wait()
    targets = [pattern[0, 0, block] for block in range(supers)]

    def block_for(target):
        found = jnp.int32(0)
        for block in range(supers):
            found = jnp.where(targets[block] == target, jnp.int32(block), found)
        return factor[found]

    def product(block):
        return times(block_for(block), inverse_packed[0])

    @pl.when(place == 0)
    def _():
        for block in range(supers):
            pack_turned(block, block_for(block))
        fresh = times_transposed(rhs[0], inverse_packed[0])
        rhs[0] = fresh
        forward_ref[...] = fresh

    @pl.when(((place > 0) & (place < below)) | ((place == below) & works))
    def _():
        for block in range(supers):
            value = product(block)
            pack(block, value)
            pack_turned(block, value)

    @pl.when((place == below) & lends)
    def _():
        for block in range(supers):
            made[block] = product(block)
            remote(lambda block=block: (made.at[block], made.at[block], made_sem, (top, mate)))
        finish()

    @pl.when(lends)
    def _():
        sends.extend(lent)
        finish()
        arrive(back, back_sem.at[0])
        forward_ref[...] = back[...]
        arrive(solved.at[0], back_sem.at[1])
        for piece in range(PIECES):
            answer_ref[piece * rows:(piece + 1) * rows, :] = solved[0, piece]

    def part_of(piece):
        return slice(piece * rows, (piece + 1) * rows)

    def spread(piece, value, level):
        wide = times_turned(value, turned[...])
        for block in range(supers):
            outbox[piece, block] = wide[:, block * width:(block + 1) * width]
        if level < below:
            scatter(
                lambda item, piece=piece: (
                    outbox.at[piece, item], inbox.at[piece, me], inbox_sem.at[piece], host(level + 1, item)
                ),
                lambda item: None,
            )
        else:
            @pl.when(works)
            def _():
                inbox_top[piece, first_id] = outbox[piece, second_id]

            scatter(
                lambda item, piece=piece: (
                    outbox.at[piece, item], inbox_top.at[piece, first_id], top_sem.at[piece], host(top, item)
                ),
                lambda item: host(top, item),
            )

    def backward(piece, source, which):
        picked = jnp.concatenate([source[block] for block in range(supers)], axis=1)
        fresh = yout[which, part_of(piece), :] - times(picked, packed[...])
        solved[which, piece] = fresh
        return fresh

    for level in range(below):
        @pl.when(place == level)
        def _():
            begin()
            for piece in range(PIECES):
                if level > 0:
                    arrive(inbox.at[piece], inbox_sem.at[piece])
                    rhs[0, part_of(piece), :] = rhs[0, part_of(piece), :] - jnp.sum(inbox[piece], axis=0)
                if piece == 0:
                    pl.semaphore_wait(barrier, supers)
                spread(piece, rhs[0, part_of(piece), :], level)
            if level > 0:
                forward_ref[...] = times_transposed(rhs[0], inverse_packed[0])
            else:
                for block in range(supers):
                    pack(block, product(block))
            yout[0] = times(forward_ref[...], inverse_packed[0])
            for piece in range(PIECES):
                arrive(arrived.at[piece], arrived_sem.at[piece])
                answer_ref[part_of(piece), :] = backward(piece, arrived.at[piece], 0)
                if level > 0:
                    scatter(
                        lambda item, piece=piece: (
                            solved.at[0, piece], arrived.at[piece, me], arrived_sem.at[piece], (level - 1, item)
                        ),
                        lambda item: None,
                    )
            finish()

    @pl.when(works)
    def _():
        begin()
        which = 1 - slot
        arrive(rhs.at[which], extra_sem.at[0])
        arrive(inverse.at[which], extra_sem.at[1])
        pack_inverse(which)
        high, low = halves(times(inverse[1].T, inverse_packed[1]))
        square[:, :width] = high
        square[:, width:] = low

        @pl.when(place == top)
        def _():
            arrive(made, made_sem)
            for block in range(supers):
                value = made[block]
                pack(block, value)
                pack_turned(block, value)

        pl.semaphore_wait(barrier, supers - 1)
        for piece in range(PIECES):
            arrive(inbox.at[piece], inbox_sem.at[piece])
            rhs[0, part_of(piece), :] = rhs[0, part_of(piece), :] - jnp.sum(inbox[piece], axis=0)
            spread(piece, rhs[0, part_of(piece), :], below)
        first = times_transposed(rhs[0], inverse_packed[0])
        yout[0] = times(first, inverse_packed[0])

        @pl.when(place == below)
        def _():
            forward_ref[...] = first

        @pl.when(place == top)
        def _():
            back[...] = first

        for piece in range(PIECES):
            arrive(inbox_top.at[piece, pl.ds(0, supers - 1)], top_sem.at[piece])
            total = rhs[1, part_of(piece), :] - jnp.sum(inbox_top[piece], axis=0)
            rhs[1, part_of(piece), :] = total
            fresh = times(total, square[...])
            solved[1, piece] = fresh
            arrived_top[piece, second_id] = fresh
            scatter(
                lambda item, piece=piece: (
                    solved.at[1, piece], arrived_top.at[piece, second_id], back_top_sem.at[piece],
                    host(below, item),
                ),
                lambda item: host(below, item),
            )
        second = times_transposed(rhs[1], inverse_packed[1])

        @pl.when(place == below)
        def _():
            back[...] = second

        @pl.when(place == top)
        def _():
            forward_ref[...] = second

        remote(lambda: (back, back, back_sem.at[0], (mate_chain, mate)))
        for piece in range(PIECES):
            arrive(arrived_top.at[piece, pl.ds(0, supers - 1)], back_top_sem.at[piece])
            backward(piece, arrived_top.at[piece], 0)
            scatter(
                lambda item, piece=piece: (
                    solved.at[0, piece], arrived.at[piece, first_id], arrived_sem.at[piece], (below - 1, item)
                ),
                lambda item: None,
            )
        remote(lambda: (solved.at[which], solved.at[0], back_sem.at[1], (mate_chain, mate)))
        for piece in range(PIECES):
            answer_ref[part_of(piece), :] = solved[slot, piece]
        finish()


def folded_body(rhs, inverse, factor, pattern):
    levels = lax.axis_size("chain")
    supers = lax.axis_size("col")
    loads, width = rhs.shape[2:]
    rows = loads // PIECES
    f32, bf16 = jnp.float32, jnp.bfloat16
    piece = (rows, width)
    dma = pltpu.SemaphoreType.DMA
    anywhere = pl.BlockSpec(memory_space=pl.ANY)
    both = pl.pallas_call(
        functools.partial(folded_kernel, levels, supers),
        out_shape=pltpu.VMEM((2, loads, width), f32),
        in_specs=[anywhere] * 4,
        out_specs=pl.BlockSpec(memory_space=pltpu.VMEM),
        scratch_shapes=[
            pltpu.VMEM((2, loads, width), f32),
            pltpu.VMEM((2, width, width), f32),
            pltpu.VMEM((supers, width, width), f32),
            pltpu.SMEM((1, 1, supers), jnp.int32),
            pltpu.VMEM((2, width, 2 * width), bf16),
            pltpu.VMEM((supers * width, 2 * width), bf16),
            pltpu.VMEM((2 * width, supers * width), bf16),
            pltpu.VMEM((width, 2 * width), bf16),
            pltpu.VMEM((supers, width, width), f32),
            pltpu.VMEM((PIECES, supers) + piece, f32),
            pltpu.VMEM((PIECES, supers) + piece, f32),
            pltpu.VMEM((PIECES, supers) + piece, f32),
            pltpu.VMEM((PIECES, supers) + piece, f32),
            pltpu.VMEM((PIECES, supers) + piece, f32),
            pltpu.VMEM((2, PIECES) + piece, f32),
            pltpu.VMEM((2, loads, width), f32),
            pltpu.VMEM((loads, width), f32),
            dma((4,)),
            dma((3 * PIECES * supers + 8,)),
            dma((PIECES,)),
            dma((PIECES,)),
            dma((PIECES,)),
            dma((PIECES,)),
            dma((2,)),
            dma(()),
            dma((2,)),
        ],
        compiler_params=pltpu.CompilerParams(collective_id=0, has_side_effects=True),
    )(rhs[0, 0], inverse[0, 0], factor[0, 0], pattern)
    return (both[None, :1], both[None, 1:])


def solution(mesh):
    levels, supers = mesh.shape["chain"], mesh.shape["col"]

    def chosen(rhs, inverse, factor, pattern):
        dense = factor.shape[2] == supers and supers % 8 == 0 and levels > 2
        return (folded_body if dense else body)(rhs, inverse, factor, pattern)

    in_specs = (
        P("chain", "col", None, None),
        P("chain", "col", None, None),
        P("chain", "col", None, None, None),
        P("chain", "col", None),
    )
    out_specs = (P("chain", "col", None, None), P("chain", "col", None, None))
    return jax.shard_map(chosen, mesh=mesh, in_specs=in_specs, out_specs=out_specs, check_vma=False)
```

```python
import functools

import jax
import jax.numpy as jnp
from jax import lax
from jax.experimental import pallas as pl
from jax.experimental.pallas import tpu as pltpu
from jax.sharding import PartitionSpec as P

PIECES = 4
MESH = pl.DeviceIdType.MESH


def halves(value):
    high = value.astype(jnp.bfloat16)
    low = (value - high.astype(jnp.float32)).astype(jnp.bfloat16)
    return high, low


def times_transposed(value, packed):
    rows = value.shape[0]
    high, low = halves(value)
    stacked = jnp.concatenate(
        [jnp.concatenate([high, low], axis=1), jnp.concatenate([low, high], axis=1)], axis=0
    )
    both = lax.dot_general(
        stacked, packed, (((1,), (1,)), ((), ())), preferred_element_type=jnp.float32
    )
    return both[:rows] + both[rows:]


def times_turned(value, turned):
    rows = value.shape[0]
    high, low = halves(value)
    stacked = jnp.concatenate(
        [jnp.concatenate([high, low], axis=1), jnp.concatenate([low, high], axis=1)], axis=0
    )
    both = jnp.dot(stacked, turned, preferred_element_type=jnp.float32)
    return both[:rows] + both[rows:]


def times(value, packed):
    rows = value.shape[0]
    width = packed.shape[1] // 2
    high, low = halves(value)
    both = jnp.dot(
        jnp.concatenate([high, low], axis=0), packed, preferred_element_type=jnp.float32
    )
    summed = both[:rows] + both[rows:]
    return summed[:, :width] + summed[:, width:]


def kernel(
    levels, supers, rhs_hbm, inverse_hbm, factor_hbm, pattern_hbm, both_ref,
    rhs, inverse, factor, pattern, inverse_packed, packed, turned, terms, outbox, inbox, solved,
    load_sem, outbox_sem, inbox_sem, solved_sem, arrived_sem, *arrived,
):
    forward_ref, answer_ref = both_ref.at[0], both_ref.at[1]
    place = lax.axis_index("chain")
    me = lax.axis_index("col")
    count, _, width = factor.shape
    loads = rhs.shape[0]
    rows = loads // PIECES
    loading = [
        pltpu.make_async_copy(source, target, load_sem.at[at])
        for at, (source, target) in enumerate(
            ((rhs_hbm, rhs), (inverse_hbm, inverse), (factor_hbm, factor), (pattern_hbm, pattern))
        )
    ]
    for copy in loading:
        copy.start()
    peers = [lax.rem(me + shift, supers) for shift in range(supers)]
    upper = lax.div(2 * me, supers)
    distant = [(1 - upper) * (supers - 1 - k) + upper * k for k in range(supers)]
    distant = [(peer, lax.rem(peer - me + supers, supers)) for peer in distant]

    barrier = pltpu.get_barrier_semaphore()

    @pl.when(place > 0)
    def _():
        for peer in peers:
            pl.semaphore_signal(
                barrier, inc=1, device_id={"chain": place - 1, "col": peer}, device_id_type=MESH
            )

    @pl.when(place < levels - 1)
    def _():
        for peer in peers:
            pl.semaphore_signal(
                barrier, inc=1, device_id={"chain": place + 1, "col": peer}, device_id_type=MESH
            )

    loading[0].wait()
    loading[1].wait()
    high, low = halves(inverse[...])
    inverse_packed[:, :width] = high
    inverse_packed[:, width:] = low

    full = count == supers

    def pack(block, value):
        high, low = halves(value)
        packed[block * width:(block + 1) * width, :width] = high
        packed[block * width:(block + 1) * width, width:] = low

    def pack_turned(block, value):
        high, low = halves(value.T)
        turned[:width, block * width:(block + 1) * width] = high
        turned[width:, block * width:(block + 1) * width] = low

    def block_of(block):
        return factor[jnp.maximum(origin[block], 0)] if full else factor[block]

    loading[2].wait()
    loading[3].wait()
    targets = [pattern[0, 0, block] for block in range(count)]
    origin = []
    for peer in peers:
        at = jnp.int32(-1)
        for block in range(count):
            at = jnp.where(targets[block] == peer, jnp.int32(block), at)
        origin.append(at)
    slots = [lax.rem(me - target + supers, supers) for target in targets]

    @pl.when(place == 0)
    def _():
        for block in range(count):
            pack_turned(block, block_of(block))
        rhs[...] = times_transposed(rhs[...], inverse_packed[...])
        forward_ref[...] = rhs[...]

    @pl.when((place > 0) & (place < levels - 1))
    def _():
        for block in range(count):
            product = times(block_of(block), inverse_packed[...])
            pack(block, product)
            pack_turned(block, product)

    @pl.when(place == levels - 1)
    def _():
        pack(0, times(inverse[...].T, inverse_packed[...]))

    def term_copy(piece, peer, shift):
        return pltpu.make_async_remote_copy(
            src_ref=outbox.at[piece, shift],
            dst_ref=inbox.at[piece, shift],
            send_sem=outbox_sem.at[piece, shift],
            recv_sem=inbox_sem.at[piece],
            device_id={"chain": place + 1, "col": peer},
            device_id_type=MESH,
        )

    def answer_copy(piece, peer, shift):
        return pltpu.make_async_remote_copy(
            src_ref=solved.at[piece],
            dst_ref=arrived[piece].at[shift],
            send_sem=solved_sem.at[piece, shift],
            recv_sem=arrived_sem.at[piece],
            device_id={"chain": place - 1, "col": peer},
            device_id_type=MESH,
        )

    for piece in range(PIECES):
        part = pl.ds(piece * rows, rows)

        @pl.when(place > 0)
        def _():
            pltpu.make_async_copy(inbox.at[piece], inbox.at[piece], inbox_sem.at[piece]).wait()
            total = rhs[part, :] - jnp.sum(inbox[piece], axis=0)
            rhs[part, :] = total

        @pl.when(place < levels - 1)
        def _():
            wide = times_turned(rhs[part, :], turned[...])
            if full:
                for shift in range(supers):
                    outbox[piece, shift] = wide[:, shift * width:(shift + 1) * width]
            else:
                for block in range(count):
                    terms[block] = wide[:, block * width:(block + 1) * width]
                for shift in range(supers):
                    picked = terms[jnp.maximum(origin[shift], 0)]
                    outbox[piece, shift] = jnp.where(origin[shift] >= 0, picked, 0.0)

        @pl.when(place == levels - 1)
        def _():
            fresh = times(rhs[part, :], packed[:width, :])
            solved[piece] = fresh
            answer_ref[part, :] = fresh

        if piece == 0:
            pl.semaphore_wait(
                barrier, jnp.where(place > 0, supers, 0) + jnp.where(place < levels - 1, supers, 0)
            )

        @pl.when(place < levels - 1)
        def _():
            for peer, shift in distant:
                term_copy(piece, peer, shift).start()

        @pl.when(place == levels - 1)
        def _():
            for peer, shift in distant:
                answer_copy(piece, peer, shift).start()

    @pl.when(place > 0)
    def _():
        forward_ref[...] = times_transposed(rhs[...], inverse_packed[...])

    @pl.when(place == 0)
    def _():
        for block in range(count):
            pack(block, times(block_of(block), inverse_packed[...]))

    @pl.when(place < levels - 1)
    def _():
        rhs[...] = times(forward_ref[...], inverse_packed[...])
        for piece in range(PIECES):
            part = pl.ds(piece * rows, rows)
            pltpu.make_async_copy(arrived[piece], arrived[piece], arrived_sem.at[piece]).wait()
            if full:
                chosen = [arrived[piece][(supers - shift) % supers] for shift in range(supers)]
            else:
                chosen = [arrived[piece][slot] for slot in slots]
            picked = jnp.concatenate(chosen, axis=1)
            fresh = rhs[part, :] - times(picked, packed[...])
            solved[piece] = fresh
            answer_ref[part, :] = fresh

            @pl.when(place > 0)
            def _():
                for peer, shift in distant:
                    answer_copy(piece, peer, shift).start()

    @pl.when(place < levels - 1)
    def _():
        for piece in range(PIECES):
            for peer, shift in distant:
                term_copy(piece, peer, shift).wait_send()

    @pl.when(place > 0)
    def _():
        for piece in range(PIECES):
            for peer, shift in distant:
                answer_copy(piece, peer, shift).wait_send()


def body(rhs, inverse, factor, pattern):
    levels = lax.axis_size("chain")
    supers = lax.axis_size("col")
    loads, width = rhs.shape[2:]
    count = factor.shape[2]
    rows = loads // PIECES
    block = pltpu.VMEM((2, loads, width), jnp.float32)
    anywhere = pl.BlockSpec(memory_space=pl.ANY)
    both = pl.pallas_call(
        functools.partial(kernel, levels, supers),
        out_shape=block,
        in_specs=[anywhere] * 4,
        out_specs=pl.BlockSpec(memory_space=pltpu.VMEM),
        scratch_shapes=[
            pltpu.VMEM((loads, width), jnp.float32),
            pltpu.VMEM((width, width), jnp.float32),
            pltpu.VMEM((count, width, width), jnp.float32),
            pltpu.SMEM((1, 1, count), jnp.int32),
            pltpu.VMEM((width, 2 * width), jnp.bfloat16),
            pltpu.VMEM((count * width, 2 * width), jnp.bfloat16),
            pltpu.VMEM((2 * width, count * width), jnp.bfloat16),
            pltpu.VMEM((count, rows, width), jnp.float32),
            pltpu.VMEM((PIECES, supers, rows, width), jnp.float32),
            pltpu.VMEM((PIECES, supers, rows, width), jnp.float32),
            pltpu.VMEM((PIECES, rows, width), jnp.float32),
            pltpu.SemaphoreType.DMA((4,)),
            pltpu.SemaphoreType.DMA((PIECES, supers)),
            pltpu.SemaphoreType.DMA((PIECES,)),
            pltpu.SemaphoreType.DMA((PIECES, supers)),
            pltpu.SemaphoreType.DMA((PIECES,)),
            *[pltpu.VMEM((supers, rows, width), jnp.float32)] * PIECES,
        ],
        compiler_params=pltpu.CompilerParams(collective_id=0, has_side_effects=True),
    )(rhs[0, 0], inverse[0, 0], factor[0, 0], pattern)
    return (both[None, :1], both[None, 1:])


def inner_kernel(
    levels, supers, rhs_hbm, inverse_hbm, factor_hbm, pattern_hbm, both_ref,
    rhs, inverse, factor, pattern, inverse_packed, packed, turned, square,
    outbox, inbox, inbox_top, arrived, solved, solved_top, back,
    load_sem, outbox_sem, inbox_sem, solved_sem, arrived_sem, top_sem, lend_sem, extra_sem, back_sem,
):
    forward_ref, answer_ref = both_ref.at[0], both_ref.at[1]
    place = lax.axis_index("chain")
    me = lax.axis_index("col")
    width = factor.shape[1]
    rows = rhs.shape[1] // PIECES
    below, top = levels - 2, levels - 1
    depth = supers // 2
    quarter = depth // 4
    z, y = lax.div(me, 2), lax.rem(me, 2)
    upper = lax.div(z, depth // 2)
    middle = lax.rem(lax.div(lax.div(z, quarter) + 1, 2), 2)
    mate = 2 * (z + (1 - 2 * middle) * quarter * (1 - 2 * upper)) + y
    works = (place == top) & (middle == 1)
    lends = (place == top) & (middle == 0)
    order = []
    for deep in range(quarter, 3 * quarter):
        for side in range(2):
            far = deep - quarter if deep < 2 * quarter else deep + quarter
            order += [2 * deep + side, 2 * far + side]
    is_below = lax.div(place, below) - lax.div(place, top)
    mine = 2 * (me - 2 * quarter)

    loading = [
        pltpu.make_async_copy(source, target, load_sem.at[at])
        for at, (source, target) in enumerate(
            (
                (rhs_hbm, rhs.at[0]), (inverse_hbm, inverse.at[0]),
                (factor_hbm, factor), (pattern_hbm, pattern),
            )
        )
    ]
    for copy in loading:
        copy.start()
    peers = [lax.rem(me + shift, supers) for shift in range(supers)]
    distant = [(1 - upper) * (supers - 1 - k) + upper * k for k in range(supers)]
    near_top = []
    for k in range(2 * quarter):
        deep = (1 - upper) * (3 * quarter - 1 - k) + upper * (quarter + k)
        for side in (1 - y, y):
            near_top.append((2 * deep + side, 2 * (2 * (deep - quarter) + side)))

    barrier = pltpu.get_barrier_semaphore()

    def greet(chain, col):
        pl.semaphore_signal(
            barrier, inc=1, device_id={"chain": chain, "col": col}, device_id_type=MESH
        )

    @pl.when(((place > 0) & (place < top)) | works)
    def _():
        for peer in peers:
            greet(place - 1, peer)

    @pl.when(works)
    def _():
        greet(top, mate)

    def lend(at):
        return pltpu.make_async_remote_copy(
            src_ref=(rhs_hbm, inverse_hbm)[at], dst_ref=(rhs, inverse)[at].at[1],
            send_sem=lend_sem.at[at], recv_sem=extra_sem.at[at],
            device_id={"chain": top, "col": mate}, device_id_type=MESH,
        )

    def give(at):
        return pltpu.make_async_remote_copy(
            src_ref=back.at[at], dst_ref=back.at[at],
            send_sem=lend_sem.at[at], recv_sem=back_sem.at[at],
            device_id={"chain": top, "col": mate}, device_id_type=MESH,
        )

    def arrive(ref, sem):
        pltpu.make_async_copy(ref, ref, sem).wait()

    @pl.when(lends)
    def _():
        pl.semaphore_wait(barrier, 1)
        for at in range(2):
            lend(at).start()

    def pack_inverse(which):
        high, low = halves(inverse[which])
        inverse_packed[which, :, :width] = high
        inverse_packed[which, :, width:] = low

    loading[0].wait()
    loading[1].wait()
    pack_inverse(0)

    def pack(block, value):
        high, low = halves(value)
        packed[block * width:(block + 1) * width, :width] = high
        packed[block * width:(block + 1) * width, width:] = low

    def pack_turned(block, value):
        high, low = halves(value.T)
        turned[:width, block * width:(block + 1) * width] = high
        turned[width:, block * width:(block + 1) * width] = low

    loading[2].wait()
    loading[3].wait()
    targets = [pattern[0, 0, block] for block in range(supers)]

    def block_of(position):
        wanted = position + (order[position] - position) * is_below
        found = jnp.int32(0)
        for block in range(supers):
            found = jnp.where(targets[block] == wanted, jnp.int32(block), found)
        return factor[found]

    @pl.when(place == 0)
    def _():
        for block in range(supers):
            pack_turned(block, block_of(block))
        fresh = times_transposed(rhs[0], inverse_packed[0])
        rhs[0] = fresh
        forward_ref[...] = fresh

    @pl.when((place > 0) & (place < top))
    def _():
        for block in range(supers):
            product = times(block_of(block), inverse_packed[0])
            pack(block, product)
            pack_turned(block, product)

    @pl.when(works)
    def _():
        for which in range(2):
            if which:
                arrive(rhs.at[1], extra_sem.at[0])
                arrive(inverse.at[1], extra_sem.at[1])
                pack_inverse(1)
            high, low = halves(times(inverse[which].T, inverse_packed[which]))
            square[which, :, :width] = high
            square[which, :, width:] = low

    def term_copy(piece, peer):
        return pltpu.make_async_remote_copy(
            src_ref=outbox.at[piece, peer], dst_ref=inbox.at[piece, me],
            send_sem=outbox_sem.at[piece, peer], recv_sem=inbox_sem.at[piece],
            device_id={"chain": place + 1, "col": peer}, device_id_type=MESH,
        )

    def top_copy(piece, col, start):
        return pltpu.make_async_remote_copy(
            src_ref=outbox.at[piece, pl.ds(start, 2)], dst_ref=inbox_top.at[piece, me],
            send_sem=outbox_sem.at[piece, start], recv_sem=top_sem.at[piece],
            device_id={"chain": top, "col": col}, device_id_type=MESH,
        )

    def answer_copy(piece, peer):
        return pltpu.make_async_remote_copy(
            src_ref=solved.at[piece], dst_ref=arrived.at[piece, me],
            send_sem=solved_sem.at[piece, peer], recv_sem=arrived_sem.at[piece],
            device_id={"chain": place - 1, "col": peer}, device_id_type=MESH,
        )

    def pair_copy(piece, peer):
        return pltpu.make_async_remote_copy(
            src_ref=solved_top.at[piece], dst_ref=arrived.at[piece, pl.ds(mine, 2)],
            send_sem=solved_sem.at[piece, peer], recv_sem=arrived_sem.at[piece],
            device_id={"chain": below, "col": peer}, device_id_type=MESH,
        )

    for piece in range(PIECES):
        part = pl.ds(piece * rows, rows)

        @pl.when((place > 0) & (place < top))
        def _():
            arrive(inbox.at[piece], inbox_sem.at[piece])
            rhs[0, part, :] = rhs[0, part, :] - jnp.sum(inbox[piece], axis=0)

        @pl.when(place < top)
        def _():
            wide = times_turned(rhs[0, part, :], turned[...])
            for block in range(supers):
                outbox[piece, block] = wide[:, block * width:(block + 1) * width]

        if piece == 0:
            @pl.when(place < top)
            def _():
                pl.semaphore_wait(barrier, supers - (supers // 2) * is_below)

        @pl.when(place < below)
        def _():
            for peer in distant:
                term_copy(piece, peer).start()

        @pl.when(place == below)
        def _():
            for col, start in near_top:
                top_copy(piece, col, start).start()

        @pl.when(works)
        def _():
            arrive(inbox_top.at[piece], top_sem.at[piece])
            for which in range(2):
                total = rhs[which, part, :] - jnp.sum(inbox_top[piece, :, which], axis=0)
                rhs[which, part, :] = total
                solved_top[piece, which] = times(total, square[which])
            for peer in distant:
                pair_copy(piece, peer).start()

    @pl.when((place > 0) & (place < top))
    def _():
        forward_ref[...] = times_transposed(rhs[0], inverse_packed[0])

    @pl.when(place == 0)
    def _():
        for block in range(supers):
            pack(block, times(block_of(block), inverse_packed[0]))

    @pl.when(place < top)
    def _():
        rhs[0] = times(forward_ref[...], inverse_packed[0])
        for piece in range(PIECES):
            part = pl.ds(piece * rows, rows)
            arrive(arrived.at[piece], arrived_sem.at[piece])
            picked = jnp.concatenate([arrived[piece, block] for block in range(supers)], axis=1)
            fresh = rhs[0, part, :] - times(picked, packed[...])
            solved[piece] = fresh
            answer_ref[part, :] = fresh

            @pl.when(place > 0)
            def _():
                for peer in distant:
                    answer_copy(piece, peer).start()

    @pl.when(works)
    def _():
        back[0] = times_transposed(rhs[1], inverse_packed[1])
        forward_ref[...] = times_transposed(rhs[0], inverse_packed[0])
        for piece in range(PIECES):
            part = pl.ds(piece * rows, rows)
            answer_ref[part, :] = solved_top[piece, 0]
            back[1, part, :] = solved_top[piece, 1]
        for at in range(2):
            give(at).start()
        for piece in range(PIECES):
            for peer in distant:
                pair_copy(piece, peer).wait_send()
        for at in range(2):
            give(at).wait_send()

    @pl.when(lends)
    def _():
        for at in range(2):
            lend(at).wait_send()
            arrive(back.at[at], back_sem.at[at])
        forward_ref[...] = back[0]
        answer_ref[...] = back[1]

    @pl.when(place < below)
    def _():
        for piece in range(PIECES):
            for peer in distant:
                term_copy(piece, peer).wait_send()

    @pl.when(place == below)
    def _():
        for piece in range(PIECES):
            for col, start in near_top:
                top_copy(piece, col, start).wait_send()

    @pl.when((place > 0) & (place < top))
    def _():
        for piece in range(PIECES):
            for peer in distant:
                answer_copy(piece, peer).wait_send()


def inner_body(rhs, inverse, factor, pattern):
    levels = lax.axis_size("chain")
    supers = lax.axis_size("col")
    loads, width = rhs.shape[2:]
    rows = loads // PIECES
    f32, bf16 = jnp.float32, jnp.bfloat16
    piece = (rows, width)
    dma = pltpu.SemaphoreType.DMA
    anywhere = pl.BlockSpec(memory_space=pl.ANY)
    both = pl.pallas_call(
        functools.partial(inner_kernel, levels, supers),
        out_shape=pltpu.VMEM((2, loads, width), f32),
        in_specs=[anywhere] * 4,
        out_specs=pl.BlockSpec(memory_space=pltpu.VMEM),
        scratch_shapes=[
            pltpu.VMEM((2, loads, width), f32),
            pltpu.VMEM((2, width, width), f32),
            pltpu.VMEM((supers, width, width), f32),
            pltpu.SMEM((1, 1, supers), jnp.int32),
            pltpu.VMEM((2, width, 2 * width), bf16),
            pltpu.VMEM((supers * width, 2 * width), bf16),
            pltpu.VMEM((2 * width, supers * width), bf16),
            pltpu.VMEM((2, width, 2 * width), bf16),
            pltpu.VMEM((PIECES, supers) + piece, f32),
            pltpu.VMEM((PIECES, supers) + piece, f32),
            pltpu.VMEM((PIECES, supers, 2) + piece, f32),
            pltpu.VMEM((PIECES, supers) + piece, f32),
            pltpu.VMEM((PIECES,) + piece, f32),
            pltpu.VMEM((PIECES, 2) + piece, f32),
            pltpu.VMEM((2, loads, width), f32),
            dma((4,)),
            dma((PIECES, supers)),
            dma((PIECES,)),
            dma((PIECES, supers)),
            dma((PIECES,)),
            dma((PIECES,)),
            dma((2,)),
            dma((2,)),
            dma((2,)),
        ],
        compiler_params=pltpu.CompilerParams(collective_id=0, has_side_effects=True),
    )(rhs[0, 0], inverse[0, 0], factor[0, 0], pattern)
    return (both[None, :1], both[None, 1:])


def solution(mesh):
    levels, supers = mesh.shape["chain"], mesh.shape["col"]

    def chosen(rhs, inverse, factor, pattern):
        dense = factor.shape[2] == supers and supers % 8 == 0 and levels > 3
        return (inner_body if dense else body)(rhs, inverse, factor, pattern)

    in_specs = (
        P("chain", "col", None, None),
        P("chain", "col", None, None),
        P("chain", "col", None, None, None),
        P("chain", "col", None),
    )
    out_specs = (P("chain", "col", None, None), P("chain", "col", None, None))
    return jax.shard_map(chosen, mesh=mesh, in_specs=in_specs, out_specs=out_specs, check_vma=False)
```

```python
import functools

import jax
import jax.numpy as jnp
from jax import lax
from jax.experimental import pallas as pl
from jax.experimental.pallas import tpu as pltpu
from jax.sharding import PartitionSpec as P

PIECES = 4
EDGES = (0, 2, 5, 8)
MESH = pl.DeviceIdType.MESH


def halves(value):
    high = value.astype(jnp.bfloat16)
    low = (value - high.astype(jnp.float32)).astype(jnp.bfloat16)
    return high, low


def times_transposed(value, packed):
    rows = value.shape[0]
    high, low = halves(value)
    stacked = jnp.concatenate(
        [jnp.concatenate([high, low], axis=1), jnp.concatenate([low, high], axis=1)], axis=0
    )
    both = lax.dot_general(
        stacked, packed, (((1,), (1,)), ((), ())), preferred_element_type=jnp.float32
    )
    return both[:rows] + both[rows:]


def times_turned(value, turned):
    rows = value.shape[0]
    high, low = halves(value)
    stacked = jnp.concatenate(
        [jnp.concatenate([high, low], axis=1), jnp.concatenate([low, high], axis=1)], axis=0
    )
    both = jnp.dot(stacked, turned, preferred_element_type=jnp.float32)
    return both[:rows] + both[rows:]


def times(value, packed):
    rows = value.shape[0]
    width = packed.shape[1] // 2
    high, low = halves(value)
    both = jnp.dot(
        jnp.concatenate([high, low], axis=0), packed, preferred_element_type=jnp.float32
    )
    summed = both[:rows] + both[rows:]
    return summed[:, :width] + summed[:, width:]


def kernel(
    levels, supers, rhs_hbm, inverse_hbm, factor_hbm, pattern_hbm, both_ref,
    rhs, inverse, factor, pattern, inverse_packed, packed, turned, terms, outbox, inbox, solved,
    load_sem, outbox_sem, inbox_sem, solved_sem, arrived_sem, *arrived,
):
    forward_ref, answer_ref = both_ref.at[0], both_ref.at[1]
    place = lax.axis_index("chain")
    me = lax.axis_index("col")
    count, _, width = factor.shape
    loads = rhs.shape[0]
    rows = loads // PIECES
    loading = [
        pltpu.make_async_copy(source, target, load_sem.at[at])
        for at, (source, target) in enumerate(
            ((rhs_hbm, rhs), (inverse_hbm, inverse), (factor_hbm, factor), (pattern_hbm, pattern))
        )
    ]
    for copy in loading:
        copy.start()
    peers = [lax.rem(me + shift, supers) for shift in range(supers)]
    upper = lax.div(2 * me, supers)
    distant = [(1 - upper) * (supers - 1 - k) + upper * k for k in range(supers)]
    distant = [(peer, lax.rem(peer - me + supers, supers)) for peer in distant]

    barrier = pltpu.get_barrier_semaphore()

    @pl.when(place > 0)
    def _():
        for peer in peers:
            pl.semaphore_signal(
                barrier, inc=1, device_id={"chain": place - 1, "col": peer}, device_id_type=MESH
            )

    @pl.when(place < levels - 1)
    def _():
        for peer in peers:
            pl.semaphore_signal(
                barrier, inc=1, device_id={"chain": place + 1, "col": peer}, device_id_type=MESH
            )

    loading[0].wait()
    loading[1].wait()
    high, low = halves(inverse[...])
    inverse_packed[:, :width] = high
    inverse_packed[:, width:] = low

    full = count == supers

    def pack(block, value):
        high, low = halves(value)
        packed[block * width:(block + 1) * width, :width] = high
        packed[block * width:(block + 1) * width, width:] = low

    def pack_turned(block, value):
        high, low = halves(value.T)
        turned[:width, block * width:(block + 1) * width] = high
        turned[width:, block * width:(block + 1) * width] = low

    def block_of(block):
        return factor[jnp.maximum(origin[block], 0)] if full else factor[block]

    loading[2].wait()
    loading[3].wait()
    targets = [pattern[0, 0, block] for block in range(count)]
    origin = []
    for peer in peers:
        at = jnp.int32(-1)
        for block in range(count):
            at = jnp.where(targets[block] == peer, jnp.int32(block), at)
        origin.append(at)
    slots = [lax.rem(me - target + supers, supers) for target in targets]

    @pl.when(place == 0)
    def _():
        for block in range(count):
            pack_turned(block, block_of(block))
        rhs[...] = times_transposed(rhs[...], inverse_packed[...])
        forward_ref[...] = rhs[...]

    @pl.when((place > 0) & (place < levels - 1))
    def _():
        for block in range(count):
            product = times(block_of(block), inverse_packed[...])
            pack(block, product)
            pack_turned(block, product)

    @pl.when(place == levels - 1)
    def _():
        pack(0, times(inverse[...].T, inverse_packed[...]))

    def term_copy(piece, peer, shift):
        return pltpu.make_async_remote_copy(
            src_ref=outbox.at[piece, shift],
            dst_ref=inbox.at[piece, shift],
            send_sem=outbox_sem.at[piece, shift],
            recv_sem=inbox_sem.at[piece],
            device_id={"chain": place + 1, "col": peer},
            device_id_type=MESH,
        )

    def answer_copy(piece, peer, shift):
        return pltpu.make_async_remote_copy(
            src_ref=solved.at[piece],
            dst_ref=arrived[piece].at[shift],
            send_sem=solved_sem.at[piece, shift],
            recv_sem=arrived_sem.at[piece],
            device_id={"chain": place - 1, "col": peer},
            device_id_type=MESH,
        )

    for piece in range(PIECES):
        part = pl.ds(piece * rows, rows)

        @pl.when(place > 0)
        def _():
            pltpu.make_async_copy(inbox.at[piece], inbox.at[piece], inbox_sem.at[piece]).wait()
            total = rhs[part, :] - jnp.sum(inbox[piece], axis=0)
            rhs[part, :] = total

        @pl.when(place < levels - 1)
        def _():
            wide = times_turned(rhs[part, :], turned[...])
            if full:
                for shift in range(supers):
                    outbox[piece, shift] = wide[:, shift * width:(shift + 1) * width]
            else:
                for block in range(count):
                    terms[block] = wide[:, block * width:(block + 1) * width]
                for shift in range(supers):
                    picked = terms[jnp.maximum(origin[shift], 0)]
                    outbox[piece, shift] = jnp.where(origin[shift] >= 0, picked, 0.0)

        @pl.when(place == levels - 1)
        def _():
            fresh = times(rhs[part, :], packed[:width, :])
            solved[piece] = fresh
            answer_ref[part, :] = fresh

        if piece == 0:
            pl.semaphore_wait(
                barrier, jnp.where(place > 0, supers, 0) + jnp.where(place < levels - 1, supers, 0)
            )

        @pl.when(place < levels - 1)
        def _():
            for peer, shift in distant:
                term_copy(piece, peer, shift).start()

        @pl.when(place == levels - 1)
        def _():
            for peer, shift in distant:
                answer_copy(piece, peer, shift).start()

    @pl.when(place > 0)
    def _():
        forward_ref[...] = times_transposed(rhs[...], inverse_packed[...])

    @pl.when(place == 0)
    def _():
        for block in range(count):
            pack(block, times(block_of(block), inverse_packed[...]))

    @pl.when(place < levels - 1)
    def _():
        rhs[...] = times(forward_ref[...], inverse_packed[...])
        for piece in range(PIECES):
            part = pl.ds(piece * rows, rows)
            pltpu.make_async_copy(arrived[piece], arrived[piece], arrived_sem.at[piece]).wait()
            if full:
                chosen = [arrived[piece][(supers - shift) % supers] for shift in range(supers)]
            else:
                chosen = [arrived[piece][slot] for slot in slots]
            picked = jnp.concatenate(chosen, axis=1)
            fresh = rhs[part, :] - times(picked, packed[...])
            solved[piece] = fresh
            answer_ref[part, :] = fresh

            @pl.when(place > 0)
            def _():
                for peer, shift in distant:
                    answer_copy(piece, peer, shift).start()

    @pl.when(place < levels - 1)
    def _():
        for piece in range(PIECES):
            for peer, shift in distant:
                term_copy(piece, peer, shift).wait_send()

    @pl.when(place > 0)
    def _():
        for piece in range(PIECES):
            for peer, shift in distant:
                answer_copy(piece, peer, shift).wait_send()


def body(rhs, inverse, factor, pattern):
    levels = lax.axis_size("chain")
    supers = lax.axis_size("col")
    loads, width = rhs.shape[2:]
    count = factor.shape[2]
    rows = loads // PIECES
    block = pltpu.VMEM((2, loads, width), jnp.float32)
    anywhere = pl.BlockSpec(memory_space=pl.ANY)
    both = pl.pallas_call(
        functools.partial(kernel, levels, supers),
        out_shape=block,
        in_specs=[anywhere] * 4,
        out_specs=pl.BlockSpec(memory_space=pltpu.VMEM),
        scratch_shapes=[
            pltpu.VMEM((loads, width), jnp.float32),
            pltpu.VMEM((width, width), jnp.float32),
            pltpu.VMEM((count, width, width), jnp.float32),
            pltpu.SMEM((1, 1, count), jnp.int32),
            pltpu.VMEM((width, 2 * width), jnp.bfloat16),
            pltpu.VMEM((count * width, 2 * width), jnp.bfloat16),
            pltpu.VMEM((2 * width, count * width), jnp.bfloat16),
            pltpu.VMEM((count, rows, width), jnp.float32),
            pltpu.VMEM((PIECES, supers, rows, width), jnp.float32),
            pltpu.VMEM((PIECES, supers, rows, width), jnp.float32),
            pltpu.VMEM((PIECES, rows, width), jnp.float32),
            pltpu.SemaphoreType.DMA((4,)),
            pltpu.SemaphoreType.DMA((PIECES, supers)),
            pltpu.SemaphoreType.DMA((PIECES,)),
            pltpu.SemaphoreType.DMA((PIECES, supers)),
            pltpu.SemaphoreType.DMA((PIECES,)),
            *[pltpu.VMEM((supers, rows, width), jnp.float32)] * PIECES,
        ],
        compiler_params=pltpu.CompilerParams(collective_id=0, has_side_effects=True),
    )(rhs[0, 0], inverse[0, 0], factor[0, 0], pattern)
    return (both[None, :1], both[None, 1:])


def inner_kernel(
    levels, supers, rhs_hbm, inverse_hbm, factor_hbm, pattern_hbm, both_ref,
    rhs, inverse, factor, pattern, inverse_packed, packed, turned, square,
    outbox, inbox, inbox_top, arrived, solved, solved_top, back,
    load_sem, outbox_sem, inbox_sem, solved_sem, arrived_sem, top_sem, lend_sem, extra_sem, back_sem,
):
    forward_ref, answer_ref = both_ref.at[0], both_ref.at[1]
    place = lax.axis_index("chain")
    me = lax.axis_index("col")
    width = factor.shape[1]
    loads = rhs.shape[1]
    edges = [loads * eighth // 8 for eighth in EDGES]
    pieces = len(edges) - 1
    below, top = levels - 2, levels - 1
    depth = supers // 2
    quarter = depth // 4
    z, y = lax.div(me, 2), lax.rem(me, 2)
    upper = lax.div(z, depth // 2)
    middle = lax.rem(lax.div(lax.div(z, quarter) + 1, 2), 2)
    mate = 2 * (z + (1 - 2 * middle) * quarter * (1 - 2 * upper)) + y
    works = (place == top) & (middle == 1)
    lends = (place == top) & (middle == 0)
    order = []
    for deep in range(quarter, 3 * quarter):
        for side in range(2):
            far = deep - quarter if deep < 2 * quarter else deep + quarter
            order += [2 * deep + side, 2 * far + side]
    is_below = lax.div(place, below) - lax.div(place, top)
    mine = 2 * (me - 2 * quarter)

    loading = [
        pltpu.make_async_copy(source, target, load_sem.at[at])
        for at, (source, target) in enumerate(
            (
                (rhs_hbm, rhs.at[0]), (inverse_hbm, inverse.at[0]),
                (factor_hbm, factor), (pattern_hbm, pattern),
            )
        )
    ]
    for copy in loading:
        copy.start()
    peers = [lax.rem(me + shift, supers) for shift in range(supers)]
    distant = []
    for k in range(depth):
        deep = (1 - upper) * (depth - 1 - k) + upper * k
        distant += [2 * deep + 1 - y, 2 * deep + y]
    near_top = []
    for k in range(2 * quarter):
        deep = (1 - upper) * (3 * quarter - 1 - k) + upper * (quarter + k)
        for side in (1 - y, y):
            near_top.append((2 * deep + side, 2 * (2 * (deep - quarter) + side)))

    barrier = pltpu.get_barrier_semaphore()

    def greet(chain, col):
        pl.semaphore_signal(
            barrier, inc=1, device_id={"chain": chain, "col": col}, device_id_type=MESH
        )

    @pl.when(((place > 0) & (place < top)) | works)
    def _():
        for peer in peers:
            greet(place - 1, peer)

    @pl.when(works)
    def _():
        greet(top, mate)

    def span(piece):
        return pl.ds(edges[piece], edges[piece + 1] - edges[piece])

    def lend(at):
        return pltpu.make_async_remote_copy(
            src_ref=(rhs_hbm, inverse_hbm)[at], dst_ref=(rhs, inverse)[at].at[1],
            send_sem=lend_sem.at[at], recv_sem=extra_sem.at[at],
            device_id={"chain": top, "col": mate}, device_id_type=MESH,
        )

    def give(at):
        return pltpu.make_async_remote_copy(
            src_ref=back.at[at], dst_ref=back.at[at],
            send_sem=lend_sem.at[at], recv_sem=back_sem.at[at],
            device_id={"chain": top, "col": mate}, device_id_type=MESH,
        )

    def arrive(ref, sem):
        pltpu.make_async_copy(ref, ref, sem).wait()

    @pl.when(lends)
    def _():
        pl.semaphore_wait(barrier, 1)
        for at in range(2):
            lend(at).start()

    def pack_inverse(which):
        high, low = halves(inverse[which])
        inverse_packed[which, :, :width] = high
        inverse_packed[which, :, width:] = low

    loading[0].wait()
    loading[1].wait()
    pack_inverse(0)

    def pack(block, value):
        high, low = halves(value)
        packed[block * width:(block + 1) * width, :width] = high
        packed[block * width:(block + 1) * width, width:] = low

    def pack_turned(block, value):
        high, low = halves(value.T)
        turned[:width, block * width:(block + 1) * width] = high
        turned[width:, block * width:(block + 1) * width] = low

    loading[2].wait()
    loading[3].wait()
    targets = [pattern[0, 0, block] for block in range(supers)]

    def block_of(position):
        wanted = position + (order[position] - position) * is_below
        found = jnp.int32(0)
        for block in range(supers):
            found = jnp.where(targets[block] == wanted, jnp.int32(block), found)
        return factor[found]

    @pl.when(place == 0)
    def _():
        for block in range(supers):
            pack_turned(block, block_of(block))
        fresh = times_transposed(rhs[0], inverse_packed[0])
        rhs[0] = fresh
        forward_ref[...] = fresh

    @pl.when((place > 0) & (place < top))
    def _():
        for block in range(supers):
            product = times(block_of(block), inverse_packed[0])
            pack(block, product)
            pack_turned(block, product)

    @pl.when(works)
    def _():
        for which in range(2):
            if which:
                arrive(rhs.at[1], extra_sem.at[0])
                arrive(inverse.at[1], extra_sem.at[1])
                pack_inverse(1)
            high, low = halves(times(inverse[which].T, inverse_packed[which]))
            square[which, :, :width] = high
            square[which, :, width:] = low

    def term_copy(piece, peer):
        return pltpu.make_async_remote_copy(
            src_ref=outbox.at[peer, span(piece)], dst_ref=inbox.at[me, span(piece)],
            send_sem=outbox_sem.at[piece, peer], recv_sem=inbox_sem.at[piece],
            device_id={"chain": place + 1, "col": peer}, device_id_type=MESH,
        )

    def top_copy(piece, col, start):
        return pltpu.make_async_remote_copy(
            src_ref=outbox.at[pl.ds(start, 2), span(piece)], dst_ref=inbox_top.at[me, :, span(piece)],
            send_sem=outbox_sem.at[piece, start], recv_sem=top_sem.at[piece],
            device_id={"chain": top, "col": col}, device_id_type=MESH,
        )

    def answer_copy(piece, peer):
        return pltpu.make_async_remote_copy(
            src_ref=solved.at[span(piece)], dst_ref=arrived.at[me, span(piece)],
            send_sem=solved_sem.at[piece, peer], recv_sem=arrived_sem.at[piece],
            device_id={"chain": place - 1, "col": peer}, device_id_type=MESH,
        )

    def pair_copy(piece, peer):
        return pltpu.make_async_remote_copy(
            src_ref=solved_top.at[:, span(piece)], dst_ref=arrived.at[pl.ds(mine, 2), span(piece)],
            send_sem=solved_sem.at[piece, peer], recv_sem=arrived_sem.at[piece],
            device_id={"chain": below, "col": peer}, device_id_type=MESH,
        )

    for piece in range(pieces):
        part = span(piece)

        @pl.when((place > 0) & (place < top))
        def _():
            arrive(inbox.at[:, part], inbox_sem.at[piece])
            rhs[0, part, :] = rhs[0, part, :] - jnp.sum(inbox[:, part, :], axis=0)

        @pl.when(place < top)
        def _():
            wide = times_turned(rhs[0, part, :], turned[...])
            for block in range(supers):
                outbox[block, part, :] = wide[:, block * width:(block + 1) * width]

        if piece == 0:
            @pl.when(place < top)
            def _():
                pl.semaphore_wait(barrier, supers - (supers // 2) * is_below)

        @pl.when(place < below)
        def _():
            for peer in distant:
                term_copy(piece, peer).start()

        @pl.when(place == below)
        def _():
            for col, start in near_top:
                top_copy(piece, col, start).start()

        @pl.when(works)
        def _():
            arrive(inbox_top.at[:, :, part], top_sem.at[piece])
            for which in range(2):
                total = rhs[which, part, :] - jnp.sum(inbox_top[:, which, part, :], axis=0)
                rhs[which, part, :] = total
                solved_top[which, part, :] = times(total, square[which])
            for peer in distant:
                pair_copy(piece, peer).start()

    @pl.when((place > 0) & (place < top))
    def _():
        forward_ref[...] = times_transposed(rhs[0], inverse_packed[0])

    @pl.when(place == 0)
    def _():
        for block in range(supers):
            pack(block, times(block_of(block), inverse_packed[0]))

    @pl.when(place < top)
    def _():
        rhs[0] = times(forward_ref[...], inverse_packed[0])
        for piece in range(pieces):
            part = span(piece)
            arrive(arrived.at[:, part], arrived_sem.at[piece])
            picked = jnp.concatenate([arrived[block, part, :] for block in range(supers)], axis=1)
            fresh = rhs[0, part, :] - times(picked, packed[...])
            solved[part, :] = fresh
            answer_ref[part, :] = fresh

            @pl.when(place > 0)
            def _():
                for peer in distant:
                    answer_copy(piece, peer).start()

    @pl.when(works)
    def _():
        back[0] = times_transposed(rhs[1], inverse_packed[1])
        forward_ref[...] = times_transposed(rhs[0], inverse_packed[0])
        for piece in range(pieces):
            part = span(piece)
            answer_ref[part, :] = solved_top[0, part, :]
            back[1, part, :] = solved_top[1, part, :]
        for at in range(2):
            give(at).start()
        for piece in range(pieces):
            for peer in distant:
                pair_copy(piece, peer).wait_send()
        for at in range(2):
            give(at).wait_send()

    @pl.when(lends)
    def _():
        for at in range(2):
            lend(at).wait_send()
            arrive(back.at[at], back_sem.at[at])
        forward_ref[...] = back[0]
        answer_ref[...] = back[1]

    @pl.when(place < below)
    def _():
        for piece in range(pieces):
            for peer in distant:
                term_copy(piece, peer).wait_send()

    @pl.when(place == below)
    def _():
        for piece in range(pieces):
            for col, start in near_top:
                top_copy(piece, col, start).wait_send()

    @pl.when((place > 0) & (place < top))
    def _():
        for piece in range(pieces):
            for peer in distant:
                answer_copy(piece, peer).wait_send()


def inner_body(rhs, inverse, factor, pattern):
    levels = lax.axis_size("chain")
    supers = lax.axis_size("col")
    loads, width = rhs.shape[2:]
    pieces = len(EDGES) - 1
    f32, bf16 = jnp.float32, jnp.bfloat16
    piece = (loads, width)
    dma = pltpu.SemaphoreType.DMA
    anywhere = pl.BlockSpec(memory_space=pl.ANY)
    both = pl.pallas_call(
        functools.partial(inner_kernel, levels, supers),
        out_shape=pltpu.VMEM((2, loads, width), f32),
        in_specs=[anywhere] * 4,
        out_specs=pl.BlockSpec(memory_space=pltpu.VMEM),
        scratch_shapes=[
            pltpu.VMEM((2, loads, width), f32),
            pltpu.VMEM((2, width, width), f32),
            pltpu.VMEM((supers, width, width), f32),
            pltpu.SMEM((1, 1, supers), jnp.int32),
            pltpu.VMEM((2, width, 2 * width), bf16),
            pltpu.VMEM((supers * width, 2 * width), bf16),
            pltpu.VMEM((2 * width, supers * width), bf16),
            pltpu.VMEM((2, width, 2 * width), bf16),
            pltpu.VMEM((supers,) + piece, f32),
            pltpu.VMEM((supers,) + piece, f32),
            pltpu.VMEM((supers, 2) + piece, f32),
            pltpu.VMEM((supers,) + piece, f32),
            pltpu.VMEM(piece, f32),
            pltpu.VMEM((2,) + piece, f32),
            pltpu.VMEM((2, loads, width), f32),
            dma((4,)),
            dma((pieces, supers)),
            dma((pieces,)),
            dma((pieces, supers)),
            dma((pieces,)),
            dma((pieces,)),
            dma((2,)),
            dma((2,)),
            dma((2,)),
        ],
        compiler_params=pltpu.CompilerParams(collective_id=0, has_side_effects=True),
    )(rhs[0, 0], inverse[0, 0], factor[0, 0], pattern)
    return (both[None, :1], both[None, 1:])


def solution(mesh):
    levels, supers = mesh.shape["chain"], mesh.shape["col"]

    def chosen(rhs, inverse, factor, pattern):
        dense = factor.shape[2] == supers and supers % 8 == 0 and rhs.shape[2] % 64 == 0 and levels > 3
        return (inner_body if dense else body)(rhs, inverse, factor, pattern)

    in_specs = (
        P("chain", "col", None, None),
        P("chain", "col", None, None),
        P("chain", "col", None, None, None),
        P("chain", "col", None),
    )
    out_specs = (P("chain", "col", None, None), P("chain", "col", None, None))
    return jax.shard_map(chosen, mesh=mesh, in_specs=in_specs, out_specs=out_specs, check_vma=False)
```
